32 devices in a mesh: tm: 8 (over y, x, core), space: 4 (over z).
Axes of the slice: x: 2, y: 2, z: 4, core: 2. Of those that a mesh axis runs over, the one named last changes fastest.
Arguments:
- start_state: float32 [6, 2048], P(None, 'space'), may hold values from -6 to 6, as said below
- fine_nodes: float32 [8, 3, 6, 2048], P('tm', None, None, 'space'), may hold values from -8 to 8, as said below
Outputs:
- new_places: float32 [8, 3, 3, 2048], P('tm', None, None, 'space')
- new_strengths: float32 [8, 3, 3, 2048], P('tm', None, None, 'space')
- next_places: float32 [8, 3, 2048], P('tm', None, 'space')
- next_strengths: float32 [8, 3, 2048], P('tm', None, 'space')
The draws below stay inside these ranges and needn't reach their ends.
Inputs may be any that keep to these rules, and one draw needn't show every extreme that they name: `start_state`: rows 0 to 2 are positions within the box from -0.5 to 0.5 give or take 0.05; the particles are numbered along a Morton (Z-order) curve of the box, so that runs of consecutive particles lie close together. `fine_nodes`: rows 0 to 2 are positions within the box from -0.5 to 0.5 give or take 0.1, numbered along the same Morton curve as start_state.
All inputs are finite; a program needn't handle non-finite values.
Results may differ from the reference program's by a relative error of at most 0.0003.
Values sent between devices are 32-bit elements; how exact they have to be, the bound alone decides.
A program may use at most 64 MiB of HBM per device.

```python
import math
import jax
import jax.numpy as jnp
from jax import lax

CLUSTER = 16
PARTICLES = 2048
SLICES = 8


def cell_coordinate(particle_index, dimension, total_bits):
    coordinate = jnp.zeros_like(particle_index)
    depth_level = 0
    for bit_place in range(dimension, total_bits, 3):
        bit_value = jnp.bitwise_and(jnp.right_shift(particle_index, bit_place), 1)
        coordinate = coordinate + jnp.left_shift(bit_value, depth_level)
        depth_level = depth_level + 1
    return (coordinate, depth_level)


def morton_places(key):
    particle_index = jnp.arange(PARTICLES, dtype=jnp.int32)
    total_bits = max(3, (PARTICLES - 1).bit_length())
    jitter = jax.random.uniform(key, (3, PARTICLES), jnp.float32)
    rows_out = []
    for dimension in range(3):
        coordinate, depth_level = cell_coordinate(particle_index, dimension, total_bits)
        rows_out.append((coordinate.astype(jnp.float32) + jitter[dimension]) / float(2 ** depth_level) - 0.5)
    return jnp.stack(rows_out)


def base_draw(key):
    keys = jax.random.split(jax.random.fold_in(key, 7), 2)
    places = morton_places(keys[0])
    strengths = jnp.clip(jax.random.normal(keys[1], (3, PARTICLES), jnp.float32), -4.0, 4.0)
    return (places, strengths)


def draw_start_state(key, part):
    places, strengths = base_draw(key)
    return jnp.concatenate([places, strengths], axis=0)


def draw_fine_nodes(key, part):
    places, strengths = base_draw(key)
    keys = jax.random.split(jax.random.fold_in(key, 13), 2)
    drift = jnp.clip(0.02 * jax.random.normal(keys[0], (SLICES, 3, 3, PARTICLES), jnp.float32), -0.1, 0.1)
    ratio = 1.0 + jnp.clip(0.1 * jax.random.normal(keys[1], (SLICES, 3, 3, PARTICLES), jnp.float32), -0.3, 0.3)
    positions = places[None, None] + drift
    moments = strengths[None, None] * ratio
    return jnp.concatenate([positions, moments], axis=2)


def setup_inputs(seed: int = 0) -> dict:
    seeds = jax.random.split(jax.random.key(seed), 3)
    return {
        "start_state": draw_start_state(jax.random.fold_in(seeds[2], 71), 0),
        "fine_nodes": draw_fine_nodes(jax.random.fold_in(seeds[2], 71), 0),
    }


core_squared = 0.01
step_length = 0.02

def cross_rows(left, right):
    return jnp.stack([left[1] * right[2] - left[2] * right[1], left[2] * right[0] - left[0] * right[2], left[0] * right[1] - left[1] * right[0]])

def tile_sums(totals, target, source):
    gap_x = target[0][:, None] - source[0][None, :]
    gap_y = target[1][:, None] - source[1][None, :]
    gap_z = target[2][:, None] - source[2][None, :]
    spread = gap_x * gap_x + gap_y * gap_y + gap_z * gap_z + core_squared
    inverse = lax.rsqrt(spread)
    factor = inverse * inverse * inverse
    steep = 3.0 * factor * inverse * inverse
    curl_x = gap_y * source[5][None, :] - gap_z * source[4][None, :]
    curl_y = gap_z * source[3][None, :] - gap_x * source[5][None, :]
    curl_z = gap_x * source[4][None, :] - gap_y * source[3][None, :]
    along = steep * (target[3][:, None] * gap_x + target[4][:, None] * gap_y + target[5][:, None] * gap_z)
    velocity = jnp.stack([lax.optimization_barrier(jnp.sum(factor * curl_x, axis=1)), lax.optimization_barrier(jnp.sum(factor * curl_y, axis=1)), lax.optimization_barrier(jnp.sum(factor * curl_z, axis=1))])
    weighted = jnp.stack([lax.optimization_barrier(jnp.sum(factor * source[3][None, :], axis=1)), lax.optimization_barrier(jnp.sum(factor * source[4][None, :], axis=1)), lax.optimization_barrier(jnp.sum(factor * source[5][None, :], axis=1))])
    stretch = jnp.stack([lax.optimization_barrier(jnp.sum(along * curl_x, axis=1)), lax.optimization_barrier(jnp.sum(along * curl_y, axis=1)), lax.optimization_barrier(jnp.sum(along * curl_z, axis=1))])
    return (totals[0] + velocity, totals[1] + weighted, totals[2] + stretch)

def block_sums(totals, target, source):
    length = source.shape[1]
    block_len = math.gcd(length, 512)
    if length == block_len:
        return tile_sums(totals, target, source)
    blocks = source.reshape(6, length // block_len, block_len).transpose(1, 0, 2)

    def scan_step(carry, block):
        return (tile_sums(carry, target, block), None)
    totals, unused = lax.scan(scan_step, totals, blocks)
    return totals

def empty_sums(target):
    zeros = jnp.zeros((3, target.shape[1]), jnp.float32)
    return (zeros, zeros, zeros)

def finish(totals, target, coupling):
    stretch = cross_rows(target[3:6], totals[1]) - totals[2]
    return -coupling * jnp.concatenate([totals[0], stretch], axis=0)

def aggregate(state):
    grouped = state.reshape(6, state.shape[1] // CLUSTER, CLUSTER)
    return jnp.concatenate([lax.optimization_barrier(jnp.mean(grouped[0:3], axis=2)), lax.optimization_barrier(jnp.sum(grouped[3:6], axis=2))], axis=0)

def reference(start_state, fine_nodes):
    coupling = 1.0 / (4.0 * math.pi * math.sqrt(PARTICLES))

    def evaluate(target, source):
        return finish(block_sums(empty_sums(target), target, source), target, coupling)

    def first_pass(node_states):
        fine_first = evaluate(node_states[0], node_states[0])
        fine_middle = evaluate(node_states[1], node_states[1])
        fine_last = evaluate(node_states[2], node_states[2])
        coarse_first = evaluate(node_states[0], aggregate(node_states[0]))
        coarse_last = evaluate(node_states[2], aggregate(node_states[2]))
        correction = step_length * ((fine_first + 4.0 * fine_middle + fine_last) / 6.0 - 0.5 * (coarse_first + coarse_last))
        return (jnp.stack([fine_first, fine_middle, fine_last]), coarse_first, coarse_last, correction)
    fine_values, coarse_firsts, coarse_lasts, corrections = lax.map(first_pass, fine_nodes)

    def chain_step(initial, inputs):
        coarse_first, coarse_last, correction = inputs
        coarse_start = evaluate(initial, aggregate(initial))
        final_state = initial + step_length * (coarse_start + 0.5 * (coarse_last - coarse_first)) + correction
        return (final_state, (initial, coarse_start, final_state))
    unused, (initials, coarse_starts, finals) = lax.scan(chain_step, start_state, (coarse_firsts, coarse_lasts, corrections))

    def second_pass(inputs):
        fine_slice, coarse_first, coarse_last, initial, coarse_start, final_state = inputs
        coarse_end = evaluate(final_state, aggregate(final_state))
        change_first = coarse_start - coarse_first
        change_last = coarse_end - coarse_last
        fixed_first = fine_slice[0] + change_first
        fixed_middle = fine_slice[1] + 0.5 * (change_first + change_last)
        fixed_last = fine_slice[2] + change_last
        sweep_first = initial
        slope_first = evaluate(sweep_first, sweep_first)
        sweep_middle = sweep_first + 0.5 * step_length * (slope_first - fixed_first) + step_length * (5.0 * fixed_first + 8.0 * fixed_middle - fixed_last) / 24.0
        slope_middle = evaluate(sweep_middle, sweep_middle)
        sweep_last = sweep_middle + 0.5 * step_length * (slope_middle - fixed_middle) + step_length * (-fixed_first + 8.0 * fixed_middle + 5.0 * fixed_last) / 24.0
        return jnp.stack([sweep_first, sweep_middle, sweep_last])
    new_nodes = lax.map(second_pass, (fine_values, coarse_firsts, coarse_lasts, initials, coarse_starts, finals))
    next_start = jnp.concatenate([start_state[None], new_nodes[:-1, 2]], axis=0)
    return (new_nodes[:, :, 0:3], new_nodes[:, :, 3:6], next_start[:, 0:3], next_start[:, 3:6])
```

```python
import functools
import math

import jax
import jax.numpy as jnp
from jax import lax
from jax.experimental import pallas as pl
from jax.experimental.pallas import tpu as pltpu
from jax.sharding import PartitionSpec as P

CLUSTER = 16

core_squared = 0.01
step_length = 0.02


def rounded(value):
    return value.astype(jnp.bfloat16).astype(jnp.float32)


def split_three(value):
    one = rounded(value)
    two = rounded(value - one)
    return one, two, rounded(value - one - two)


def split_two(value):
    high = value.astype(jnp.bfloat16)
    return high, (value - high.astype(jnp.float32)).astype(jnp.bfloat16)


def product(left, right):
    return jnp.dot(left, right, preferred_element_type=jnp.float32)


def pad_rows(value):
    return jnp.concatenate([value, jnp.zeros((8 - value.shape[0], value.shape[1]), value.dtype)], axis=0)


def place_parts(state, extra):
    high = rounded(state[0:3])
    low = rounded(state[0:3] - high)
    used = high + low
    norm = used[0:1] * used[0:1] + used[1:2] * used[1:2] + used[2:3] * used[2:3] + extra
    return high, low, split_three(norm)


def source_places(state):
    high, low, norm = place_parts(state, 0.0)
    ones = jnp.ones_like(norm[0])
    none = jnp.zeros_like(norm[0])
    return jnp.concatenate(
        [high, norm[0], norm[1], norm[2], ones, ones]
        + [low, ones, none, none, none, none]
        + [high, none, none, none, none, none]
        + [low, none, none, none, none, none],
        axis=0,
    ).astype(jnp.bfloat16)


def target_places(state):
    high, low, norm = place_parts(state, core_squared)
    high = -2.0 * high
    low = -2.0 * low
    ones = jnp.ones_like(norm[0])
    none = jnp.zeros_like(norm[0])
    return jnp.concatenate(
        [high, ones, ones, ones, norm[0], norm[1]]
        + [high, norm[2], none, none, none, none]
        + [low, none, none, none, none, none]
        + [low, none, none, none, none, none],
        axis=0,
    ).astype(jnp.bfloat16)


def cross(left, right):
    return jnp.concatenate(
        [
            left[1:2] * right[2:3] - left[2:3] * right[1:2],
            left[2:3] * right[0:1] - left[0:1] * right[2:3],
            left[0:1] * right[1:2] - left[1:2] * right[0:1],
        ],
        axis=0,
    )


def source_moments(state):
    base = pad_rows(jnp.concatenate([state[3:6], cross(state[0:3], state[3:6])], axis=0))
    whole = jnp.concatenate([base, state[0:1] * base, state[1:2] * base, state[2:3] * base], axis=0)
    high, low = split_two(whole)
    for_q = jnp.concatenate([high[0:8], low[0:8]], axis=0)
    for_h = jnp.concatenate([high, low], axis=0)
    return for_q, for_h


def pair_sums(places, for_q, for_h, target, both=True):
    length = places.shape[1]
    piece = math.gcd(length, 256)
    parts_q, parts_h = [], []
    left_q, left_h = [], []
    for begin in range(0, length, piece):
        part = slice(begin, begin + piece)
        spread = lax.dot_general(
            places[:, part], target, (((0,), (0,)), ((), ())), preferred_element_type=jnp.float32
        )
        inverse = lax.rsqrt(spread)
        square = inverse * inverse
        factor = square * inverse
        steep = factor * square
        if both:
            parts_q.extend(split_two(factor))
            parts_h.extend(split_two(steep))
            left_q.extend([for_q[:, part]] * 2)
            left_h.extend([for_h[:, part]] * 2)
        else:
            parts_q.append(factor.astype(jnp.bfloat16))
            parts_h.append(steep.astype(jnp.bfloat16))
            left_q.append(for_q[:, part])
            left_h.append(for_h[:, part])

    def total(left, right):
        return product(jnp.concatenate(left, axis=1), jnp.concatenate(right, axis=0))

    got_q = total(left_q, parts_q)
    got_h = total(left_h, parts_h)
    return jnp.concatenate([got_q[0:8] + got_q[8:16], got_h[0:32] + got_h[32:64]], axis=0)


def finish(sums, state, coupling):
    places = state[0:3]
    strengths = state[3:6]
    weighted = sums[0:3]
    velocity = cross(places, weighted) - sums[3:6]
    along = (
        strengths[0:1] * places[0:1] + strengths[1:2] * places[1:2] + strengths[2:3] * places[2:3]
    )
    moment = 3.0 * (
        along * sums[8:16]
        - strengths[0:1] * sums[16:24]
        - strengths[1:2] * sums[24:32]
        - strengths[2:3] * sums[32:40]
    )
    stretch = cross(strengths, weighted) - (cross(places, moment[0:3]) - moment[3:6])
    return -coupling * jnp.concatenate([velocity, stretch], axis=0)


def kernel(
    n_t,
    n_s,
    start_ref,
    nodes_ref,
    places_out,
    strengths_out,
    next_places_out,
    next_strengths_out,
    gathered,
    sums,
    steps,
    history,
    coarse,
    middles,
    handed,
    pool,
    spots,
    send_a,
    recv_a,
    send_b,
    recv_b,
    send_d,
    recv_d,
    send_e,
    recv_e,
    send_w,
    recv_w,
    send_h,
    recv_h,
):
    length = start_ref.shape[1]
    coupling = 1.0 / (4.0 * math.pi * math.sqrt(length * n_s))
    mine = lax.axis_index("tm")
    me = lax.axis_index("space")

    def space_copy(source, target, send, recv, peer):
        return pltpu.make_async_remote_copy(
            src_ref=source, dst_ref=target, send_sem=send, recv_sem=recv,
            device_id={"space": peer}, device_id_type=pl.DeviceIdType.MESH,
        )

    def time_copy(source, target, send, recv, peer):
        return pltpu.make_async_remote_copy(
            src_ref=source, dst_ref=target, send_sem=send, recv_sem=recv,
            device_id={"tm": peer}, device_id_type=pl.DeviceIdType.MESH,
        )

    lanes = nodes_ref.shape[1]
    pieces = length // lanes

    def put(target, row, value):
        for one in range(value.shape[0]):
            for piece in range(pieces):
                target[row + one, piece : piece + 1, :] = value[
                    one : one + 1, piece * lanes : (piece + 1) * lanes
                ]

    barrier = pltpu.get_barrier_semaphore()
    for offset in range(1, n_s):
        pl.semaphore_signal(
            barrier, inc=1, device_id={"space": lax.rem(me + offset, n_s)},
            device_id_type=pl.DeviceIdType.MESH,
        )
    for offset in range(1, n_t):
        pl.semaphore_signal(
            barrier, inc=1, device_id={"tm": lax.rem(mine + offset, n_t)},
            device_id_type=pl.DeviceIdType.MESH,
        )
    for node in range(3):
        for row in range(6):
            for piece in range(pieces):
                at = (node * 6 + row) * pieces + piece
                gathered[me, node, row : row + 1, piece * lanes : (piece + 1) * lanes] = nodes_ref[
                    at : at + 1, :
                ]
    pl.semaphore_wait(barrier, n_s - 1 + n_t - 1)

    def node_copy(offset, slot):
        return space_copy(
            gathered.at[me], gathered.at[slot], send_a.at[offset], recv_a.at[offset],
            lax.rem(me + offset, n_s),
        )

    def start_copy(offset, slot):
        return space_copy(
            start_ref, history.at[0, slot], send_b.at[offset], recv_b.at[offset],
            lax.rem(me + offset, n_s),
        )

    for offset in range(1, n_s):
        node_copy(offset, me).start()
    for offset in range(1, n_s):
        start_copy(offset, me).start()
    history[0, me] = start_ref[...]

    total = n_s * length
    clusters = total // CLUSTER
    particle = lax.broadcasted_iota(jnp.int32, (total, clusters), 0)
    cluster = lax.broadcasted_iota(jnp.int32, (total, clusters), 1)
    offset_in = particle - cluster * CLUSTER
    pool[...] = jnp.where((offset_in >= 0) & (offset_in < CLUSTER), 1.0, 0.0).astype(jnp.bfloat16)

    def aggregate(blocks):
        state = pad_rows(jnp.concatenate(blocks, axis=1))
        parts = jnp.concatenate(split_three(state), axis=0).astype(jnp.bfloat16)
        got = jnp.dot(parts, pool[...], preferred_element_type=jnp.float32)
        whole = got[0:8] + got[8:16] + got[16:24]
        return jnp.concatenate([whole[0:3] * (1.0 / CLUSTER), whole[3:6]], axis=0)

    def coarse_sources(blocks):
        merged = aggregate(blocks)
        return (source_places(merged),) + source_moments(merged)

    def fine_sums(source, target, both=True):
        for_q, for_h = source_moments(source)
        return pair_sums(source_places(source), for_q, for_h, target_places(target), both)

    targets = [target_places(gathered[me, node]) for node in range(3)]
    for node in range(3):
        spots[node] = targets[node]
    for offset in range(n_s):
        source = lax.rem(me + n_s - offset, n_s)
        if offset > 0:
            node_copy(offset, source).wait_recv()
        for node in range(3):
            state = gathered[source, node]
            got = pair_sums(source_places(state), *source_moments(state), spots[node], node == 1)
            if offset == 0:
                sums[node] = got
            else:
                sums[node] = sums[node] + got

    fine = [finish(sums[node], gathered[me, node], coupling) for node in range(3)]

    def coarse_value(blocks, target, both):
        return finish(pair_sums(*coarse_sources(blocks), target_places(target), both), target, coupling)

    coarse_first = coarse_value([gathered[z, 0] for z in range(n_s)], gathered[me, 0], True)
    steps[mine, me] = step_length * ((fine[0] + 4.0 * fine[1] + fine[2]) / 6.0 - coarse_first)

    def step_copy(offset, slot):
        return space_copy(
            steps.at[mine, me], steps.at[mine, slot], send_d.at[offset], recv_d.at[offset],
            lax.rem(me + offset, n_s),
        )

    for offset in range(1, n_s):
        step_copy(offset, me).start()
    for offset in range(1, n_s):
        start_copy(offset, lax.rem(me + n_s - offset, n_s)).wait_recv()
    coarse_last = coarse_value([gathered[z, 2] for z in range(n_s)], gathered[me, 2], False)

    def coarse_step(step):
        sources = coarse_sources([history[step, z] for z in range(n_s)])

        def one_block(z, inner):
            state = history[step, z]
            coarse[step, z] = finish(pair_sums(*sources, target_places(state)), state, coupling)
            return inner

        lax.fori_loop(0, n_s, one_block, 0, unroll=math.gcd(n_s, 4))

    def advance(step):
        for z in range(n_s):
            history[step + 1, z] = history[step, z] + step_length * coarse[step, z] + steps[step, z]

    coarse_step(0)
    for offset in range(1, n_s):
        step_copy(offset, lax.rem(me + n_s - offset, n_s)).wait_recv()

    def slice_copy(offset, slot):
        return time_copy(
            steps.at[slot], steps.at[slot], send_e.at[offset], recv_e.at[offset],
            lax.rem(mine + offset, n_t),
        )

    for offset in range(1, n_t):

        @pl.when(mine + offset < n_t)
        def _():
            slice_copy(offset, mine).start()

    def chain_step(step, carry):
        slice_copy(mine - step, step).wait_recv()
        advance(step)
        coarse_step(step + 1)
        return carry

    lax.fori_loop(0, mine, chain_step, 0)
    advance(mine)

    initial = history[mine, me]
    final_state = history[mine + 1, me]
    coarse_end = coarse_value([history[mine + 1, z] for z in range(n_s)], final_state, False)
    change_first = coarse[mine, me] - coarse_first
    change_last = coarse_end - coarse_last
    fixed_first = fine[0] + change_first
    fixed_middle = fine[1] + 0.5 * (change_first + change_last)
    fixed_last = fine[2] + change_last

    sums[0] = jnp.zeros(sums.shape[1:], jnp.float32)

    def initial_block(z, carry):
        sums[0] = sums[0] + fine_sums(history[mine, z], history[mine, me], False)
        return carry

    lax.fori_loop(0, n_s, initial_block, 0)
    slope_first = finish(sums[0], initial, coupling)
    sweep_middle = (
        initial
        + 0.5 * step_length * (slope_first - fixed_first)
        + step_length * (5.0 * fixed_first + 8.0 * fixed_middle - fixed_last) / 24.0
    )
    middles[me] = sweep_middle

    def middle_copy(offset, slot):
        return space_copy(
            middles.at[me], middles.at[slot], send_w.at[offset], recv_w.at[offset],
            lax.rem(me + offset, n_s),
        )

    for offset in range(1, n_s):
        middle_copy(offset, me).start()
    put(places_out, 0, initial[0:3])
    put(strengths_out, 0, initial[3:6])
    put(places_out, 3, sweep_middle[0:3])
    put(strengths_out, 3, sweep_middle[3:6])
    sums[1] = fine_sums(sweep_middle, sweep_middle, False)
    for offset in range(1, n_s):
        source = lax.rem(me + n_s - offset, n_s)
        middle_copy(offset, source).wait_recv()
        sums[1] = sums[1] + fine_sums(middles[source], sweep_middle, False)
    slope_middle = finish(sums[1], sweep_middle, coupling)
    sweep_last = (
        sweep_middle
        + 0.5 * step_length * (slope_middle - fixed_middle)
        + step_length * (-fixed_first + 8.0 * fixed_middle + 5.0 * fixed_last) / 24.0
    )
    put(handed.at[0], 0, sweep_last)

    def last_copy():
        return time_copy(handed.at[0], handed.at[1], send_h, recv_h, lax.rem(mine + 1, n_t))

    @pl.when(mine < n_t - 1)
    def _():
        last_copy().start()

    places_out[6:9] = handed[0, 0:3]
    strengths_out[6:9] = handed[0, 3:6]
    for offset in range(1, n_s):
        node_copy(offset, me).wait_send()
        start_copy(offset, me).wait_send()
        step_copy(offset, me).wait_send()
        middle_copy(offset, me).wait_send()
    for offset in range(1, n_t):

        @pl.when(mine + offset < n_t)
        def _():
            slice_copy(offset, mine).wait_send()


    @pl.when(mine == 0)
    def _():
        put(next_places_out, 0, start_ref[0:3])
        put(next_strengths_out, 0, start_ref[3:6])

    @pl.when(mine > 0)
    def _():
        last_copy().wait_recv()
        next_places_out[...] = handed[1, 0:3]
        next_strengths_out[...] = handed[1, 3:6]

    @pl.when(mine < n_t - 1)
    def _():
        last_copy().wait_send()


def solution(mesh):
    n_t, n_s = mesh.shape["tm"], mesh.shape["space"]

    def shards(start_state, fine_nodes):
        length = start_state.shape[1]
        total = length * n_s
        vmem = pl.BlockSpec(memory_space=pltpu.VMEM)
        dma = pltpu.SemaphoreType.DMA
        lanes = math.gcd(length, 128)
        rows = (length // lanes, lanes)
        results = pl.pallas_call(
            functools.partial(kernel, n_t, n_s),
            out_shape=(
                jax.ShapeDtypeStruct((9,) + rows, jnp.float32),
                jax.ShapeDtypeStruct((9,) + rows, jnp.float32),
                jax.ShapeDtypeStruct((3,) + rows, jnp.float32),
                jax.ShapeDtypeStruct((3,) + rows, jnp.float32),
            ),
            in_specs=[vmem, vmem],
            out_specs=(vmem, vmem, vmem, vmem),
            scratch_shapes=[
                pltpu.VMEM((n_s, 3, 6, length), jnp.float32),
                pltpu.VMEM((3, 40, length), jnp.float32),
                pltpu.VMEM((n_t, n_s, 6, length), jnp.float32),
                pltpu.VMEM((n_t + 1, n_s, 6, length), jnp.float32),
                pltpu.VMEM((n_t, n_s, 6, length), jnp.float32),
                pltpu.VMEM((n_s, 6, length), jnp.float32),
                pltpu.VMEM((2, 6) + rows, jnp.float32),
                pltpu.VMEM((total, total // CLUSTER), jnp.bfloat16),
                pltpu.VMEM((3, 32, length), jnp.bfloat16),
                dma((n_s,)), dma((n_s,)),
                dma((n_s,)), dma((n_s,)),
                dma((n_s,)), dma((n_s,)),
                dma((n_t,)), dma((n_t,)),
                dma((n_s,)), dma((n_s,)),
                dma, dma,
            ],
            compiler_params=pltpu.CompilerParams(collective_id=0, has_side_effects=True),
        )(start_state, fine_nodes.reshape(-1, lanes))
        nodes, ends = (1, 3, 3, length), (1, 3, length)
        return tuple(
            one.reshape(shape) for one, shape in zip(results, (nodes, nodes, ends, ends))
        )

    return jax.shard_map(
        shards,
        mesh=mesh,
        in_specs=(P(None, "space"), P("tm", None, None, "space")),
        out_specs=(
            P("tm", None, None, "space"),
            P("tm", None, None, "space"),
            P("tm", None, "space"),
            P("tm", None, "space"),
        ),
        check_vma=False,
    )
```

```python
import functools
import math

import jax
import jax.numpy as jnp
from jax import lax
from jax.experimental import pallas as pl
from jax.experimental.pallas import tpu as pltpu
from jax.sharding import PartitionSpec as P

CLUSTER = 16

core_squared = 0.01
step_length = 0.02


def rounded(value):
    return value.astype(jnp.bfloat16).astype(jnp.float32)


def split_three(value):
    one = rounded(value)
    two = rounded(value - one)
    return one, two, rounded(value - one - two)


def split_two(value):
    high = value.astype(jnp.bfloat16)
    return high, (value - high.astype(jnp.float32)).astype(jnp.bfloat16)


def product(left, right):
    return jnp.dot(left, right, preferred_element_type=jnp.float32)


def pad_rows(value):
    return jnp.concatenate([value, jnp.zeros((8 - value.shape[0], value.shape[1]), value.dtype)], axis=0)


def place_parts(state, extra):
    high = rounded(state[0:3])
    low = rounded(state[0:3] - high)
    used = high + low
    norm = used[0:1] * used[0:1] + used[1:2] * used[1:2] + used[2:3] * used[2:3] + extra
    return high, low, split_three(norm)


def source_places(state):
    high, low, norm = place_parts(state, 0.0)
    ones = jnp.ones_like(norm[0])
    none = jnp.zeros_like(norm[0])
    return jnp.concatenate(
        [high, norm[0], norm[1], norm[2], ones, ones]
        + [low, ones, none, none, none, none]
        + [high, none, none, none, none, none]
        + [low, none, none, none, none, none],
        axis=0,
    ).astype(jnp.bfloat16)


def target_places(state):
    high, low, norm = place_parts(state, core_squared)
    high = -2.0 * high
    low = -2.0 * low
    ones = jnp.ones_like(norm[0])
    none = jnp.zeros_like(norm[0])
    return jnp.concatenate(
        [high, ones, ones, ones, norm[0], norm[1]]
        + [high, norm[2], none, none, none, none]
        + [low, none, none, none, none, none]
        + [low, none, none, none, none, none],
        axis=0,
    ).astype(jnp.bfloat16)


def cross(left, right):
    return jnp.concatenate(
        [
            left[1:2] * right[2:3] - left[2:3] * right[1:2],
            left[2:3] * right[0:1] - left[0:1] * right[2:3],
            left[0:1] * right[1:2] - left[1:2] * right[0:1],
        ],
        axis=0,
    )


def source_moments(state):
    base = pad_rows(jnp.concatenate([state[3:6], cross(state[0:3], state[3:6])], axis=0))
    whole = jnp.concatenate([base, state[0:1] * base, state[1:2] * base, state[2:3] * base], axis=0)
    high, low = split_two(whole)
    for_q = jnp.concatenate([high[0:8], low[0:8]], axis=0)
    for_h = jnp.concatenate([high, low], axis=0)
    return for_q, for_h


def pair_sums(places, for_q, for_h, target, both=True):
    length = places.shape[1]
    piece = math.gcd(length, 256)
    parts_q, parts_h = [], []
    left_q, left_h = [], []
    for begin in range(0, length, piece):
        part = slice(begin, begin + piece)
        spread = lax.dot_general(
            places[:, part], target, (((0,), (0,)), ((), ())), preferred_element_type=jnp.float32
        )
        inverse = lax.rsqrt(spread)
        square = inverse * inverse
        factor = square * inverse
        steep = factor * square
        if both:
            parts_q.extend(split_two(factor))
            parts_h.extend(split_two(steep))
            left_q.extend([for_q[:, part]] * 2)
            left_h.extend([for_h[:, part]] * 2)
        else:
            parts_q.append(factor.astype(jnp.bfloat16))
            parts_h.append(steep.astype(jnp.bfloat16))
            left_q.append(for_q[:, part])
            left_h.append(for_h[:, part])

    def total(left, right):
        return product(jnp.concatenate(left, axis=1), jnp.concatenate(right, axis=0))

    got_q = total(left_q, parts_q)
    got_h = total(left_h, parts_h)
    return jnp.concatenate([got_q[0:8] + got_q[8:16], got_h[0:32] + got_h[32:64]], axis=0)


def finish(sums, state, coupling):
    places = state[0:3]
    strengths = state[3:6]
    weighted = sums[0:3]
    velocity = cross(places, weighted) - sums[3:6]
    along = (
        strengths[0:1] * places[0:1] + strengths[1:2] * places[1:2] + strengths[2:3] * places[2:3]
    )
    moment = 3.0 * (
        along * sums[8:16]
        - strengths[0:1] * sums[16:24]
        - strengths[1:2] * sums[24:32]
        - strengths[2:3] * sums[32:40]
    )
    stretch = cross(strengths, weighted) - (cross(places, moment[0:3]) - moment[3:6])
    return -coupling * jnp.concatenate([velocity, stretch], axis=0)


def kernel(
    n_t,
    n_s,
    start_ref,
    nodes_ref,
    places_out,
    strengths_out,
    next_places_out,
    next_strengths_out,
    gathered,
    begin,
    sums,
    steps,
    history,
    coarse,
    middles,
    handed,
    pool,
    spots,
    send_a,
    recv_a,
    send_b,
    recv_b,
    send_e,
    recv_e,
    send_w,
    recv_w,
    send_h,
    recv_h,
):
    length = start_ref.shape[1]
    coupling = 1.0 / (4.0 * math.pi * math.sqrt(length * n_s))
    mine = lax.axis_index("tm")
    me = lax.axis_index("space")
    lanes = nodes_ref.shape[1]
    pieces = length // lanes
    rows = 6 * pieces

    def remote(source, target, send, recv, device):
        return pltpu.make_async_remote_copy(
            src_ref=source, dst_ref=target, send_sem=send, recv_sem=recv,
            device_id=device, device_id_type=pl.DeviceIdType.MESH,
        )

    def load(ref, base=0, count=6):
        return jnp.concatenate(
            [ref[pl.ds(base + piece, count, stride=pieces), :] for piece in range(pieces)], axis=1
        )

    def put(ref, base, value):
        for piece in range(pieces):
            ref[pl.ds(base + piece, value.shape[0], stride=pieces), :] = value[
                :, piece * lanes : (piece + 1) * lanes
            ]

    def near(rank):
        left, right = me, n_s - 1 - me
        both_sides = jnp.minimum(left, right)
        inner = rank <= 2 * both_sides
        distance = jnp.where(inner, (rank + 1) // 2, rank - both_sides)
        leftward = jnp.where(inner, rank % 2 == 1, left > right)
        return jnp.where(leftward, me - distance, me + distance)

    peers = [near(rank) for rank in range(1, n_s)]

    barrier = pltpu.get_barrier_semaphore()
    for offset in range(1, n_s):
        pl.semaphore_signal(
            barrier, inc=1, device_id={"space": lax.rem(me + offset, n_s)},
            device_id_type=pl.DeviceIdType.MESH,
        )
    for turn in range(1, n_t):
        for offset in range(n_s):
            pl.semaphore_signal(
                barrier, inc=1,
                device_id={"tm": lax.rem(mine + turn, n_t), "space": lax.rem(me + offset, n_s)},
                device_id_type=pl.DeviceIdType.MESH,
            )
    put(begin.at[me], 0, start_ref[...])
    pl.semaphore_wait(barrier, n_s * n_t - 1)

    def node_copy(peer, slot):
        return remote(nodes_ref, gathered.at[slot], send_a.at[peer], recv_a.at[slot], {"space": peer})

    def start_copy(peer, slot):
        return remote(begin.at[me], begin.at[slot], send_b.at[peer], recv_b.at[slot], {"space": peer})

    for peer in reversed(peers):
        node_copy(peer, me).start()
    for peer in reversed(peers):
        start_copy(peer, me).start()

    total = n_s * length
    clusters = total // CLUSTER
    particle = lax.broadcasted_iota(jnp.int32, (total, clusters), 0)
    cluster = lax.broadcasted_iota(jnp.int32, (total, clusters), 1)
    offset_in = particle - cluster * CLUSTER
    pool[...] = jnp.where((offset_in >= 0) & (offset_in < CLUSTER), 1.0, 0.0).astype(jnp.bfloat16)

    def aggregate(blocks):
        state = pad_rows(jnp.concatenate(blocks, axis=1))
        parts = jnp.concatenate(split_three(state), axis=0).astype(jnp.bfloat16)
        got = jnp.dot(parts, pool[...], preferred_element_type=jnp.float32)
        whole = got[0:8] + got[8:16] + got[16:24]
        return jnp.concatenate([whole[0:3] * (1.0 / CLUSTER), whole[3:6]], axis=0)

    def coarse_sources(blocks):
        merged = aggregate(blocks)
        return (source_places(merged),) + source_moments(merged)

    own = [load(nodes_ref, node * rows) for node in range(3)]
    for node in range(3):
        spots[node] = target_places(own[node])
    for rank in range(n_s):
        if rank > 0:
            source = peers[rank - 1]
            node_copy(source, source).wait_recv()
        for node in range(3):
            if rank > 0:
                state = load(gathered.at[source], node * rows)
            else:
                state = own[node]
            got = pair_sums(source_places(state), *source_moments(state), spots[node], node == 1)
            if rank == 0:
                sums[node] = got
            else:
                sums[node] = sums[node] + got

    def node_blocks(node):
        return [load(nodes_ref, node * rows)] + [load(gathered.at[peer], node * rows) for peer in peers]

    fine = [finish(sums[node], load(nodes_ref, node * rows), coupling) for node in range(3)]

    def coarse_value(blocks, target, both):
        return finish(pair_sums(*coarse_sources(blocks), target_places(target), both), target, coupling)

    coarse_first = coarse_value(node_blocks(0), load(nodes_ref, 0), True)
    put(
        steps.at[mine, me], 0,
        step_length * ((fine[0] + 4.0 * fine[1] + fine[2]) / 6.0 - coarse_first),
    )

    def step_copy(turn, peer, slice_in, place_in):
        return remote(
            steps.at[slice_in, place_in], steps.at[slice_in, place_in],
            send_e.at[turn, peer], recv_e.at[slice_in, place_in], {"tm": turn, "space": peer},
        )

    def hand_out():
        def to_slice(count, carry):
            turn = n_t - 1 - count
            for peer in peers:
                step_copy(turn, peer, mine, me).start()
            step_copy(turn, me, mine, me).start()
            return carry

        lax.fori_loop(0, n_t - 1 - mine, to_slice, 0)
        for peer in peers:
            step_copy(mine, peer, mine, me).start()

    early = n_t // 4

    @pl.when(mine < early)
    def _():
        hand_out()

    def coarse_step(step):
        sources = coarse_sources([history[step, z] for z in range(n_s)])

        def one_block(z, inner):
            state = history[step, z]
            coarse[step, z] = finish(pair_sums(*sources, target_places(state)), state, coupling)
            return inner

        lax.fori_loop(0, n_s, one_block, 0, unroll=math.gcd(n_s, 4))

    def advance(step):
        for z in range(n_s):
            history[step + 1, z] = (
                history[step, z] + step_length * coarse[step, z] + load(steps.at[step, z])
            )

    for peer in peers:
        start_copy(peer, peer).wait_recv()
    for z in range(n_s):
        history[0, z] = load(begin.at[z])
    coarse_last = coarse_value(node_blocks(2), load(nodes_ref, 2 * rows), False)

    @pl.when(mine >= early)
    def _():
        hand_out()

    coarse_step(0)

    def chain_step(step, carry):
        for z in range(n_s):
            step_copy(mine, me, step, z).wait_recv()
        advance(step)
        coarse_step(step + 1)
        return carry

    lax.fori_loop(0, mine, chain_step, 0)
    for peer in peers:
        step_copy(mine, me, mine, peer).wait_recv()
    advance(mine)

    initial = history[mine, me]
    final_state = history[mine + 1, me]
    coarse_end = coarse_value([history[mine + 1, z] for z in range(n_s)], final_state, False)
    change_first = coarse[mine, me] - coarse_first
    change_last = coarse_end - coarse_last
    fixed_first = fine[0] + change_first
    fixed_middle = fine[1] + 0.5 * (change_first + change_last)
    fixed_last = fine[2] + change_last

    def fine_sums(state, spot):
        return pair_sums(source_places(state), *source_moments(state), spot, False)

    spot = target_places(initial)
    got = fine_sums(history[mine, 0], spot)
    for z in range(1, n_s):
        got = got + fine_sums(history[mine, z], spot)
    slope_first = finish(got, initial, coupling)
    sweep_middle = (
        initial
        + 0.5 * step_length * (slope_first - fixed_first)
        + step_length * (5.0 * fixed_first + 8.0 * fixed_middle - fixed_last) / 24.0
    )
    put(middles.at[me], 0, sweep_middle)

    def middle_copy(peer, slot):
        return remote(middles.at[me], middles.at[slot], send_w.at[peer], recv_w.at[slot], {"space": peer})

    for peer in reversed(peers):
        middle_copy(peer, me).start()
    put(places_out, 0, initial[0:3])
    put(strengths_out, 0, initial[3:6])
    put(places_out, 3 * pieces, sweep_middle[0:3])
    put(strengths_out, 3 * pieces, sweep_middle[3:6])
    spot = target_places(sweep_middle)
    sums[1] = fine_sums(sweep_middle, spot)
    for peer in peers:
        middle_copy(peer, peer).wait_recv()
        sums[1] = sums[1] + fine_sums(load(middles.at[peer]), spot)
    slope_middle = finish(sums[1], sweep_middle, coupling)
    sweep_last = (
        sweep_middle
        + 0.5 * step_length * (slope_middle - fixed_middle)
        + step_length * (-fixed_first + 8.0 * fixed_middle + 5.0 * fixed_last) / 24.0
    )
    put(handed.at[0], 0, sweep_last)

    def last_copy():
        return remote(handed.at[0], handed.at[1], send_h, recv_h, {"tm": lax.rem(mine + 1, n_t)})

    @pl.when(mine < n_t - 1)
    def _():
        last_copy().start()

    half = 3 * pieces
    put(places_out, 2 * half, sweep_last[0:3])
    put(strengths_out, 2 * half, sweep_last[3:6])
    for peer in peers:
        node_copy(peer, me).wait_send()
        start_copy(peer, me).wait_send()
        middle_copy(peer, me).wait_send()
        step_copy(mine, peer, mine, me).wait_send()

    def sent(turn, carry):
        for peer in range(n_s):
            step_copy(turn, peer, mine, me).wait_send()
        return carry

    lax.fori_loop(mine + 1, n_t, sent, 0)

    @pl.when(mine == 0)
    def _():
        put(next_places_out, 0, start_ref[0:3])
        put(next_strengths_out, 0, start_ref[3:6])

    @pl.when(mine > 0)
    def _():
        last_copy().wait_recv()
        next_places_out[...] = handed[1, 0:half]
        next_strengths_out[...] = handed[1, half : 2 * half]

    @pl.when(mine < n_t - 1)
    def _():
        last_copy().wait_send()


def pass_on(*refs):
    count = len(refs) // 2
    for source, target in zip(refs[:count], refs[count:]):
        target[...] = source[...]


def solution(mesh):
    n_t, n_s = mesh.shape["tm"], mesh.shape["space"]

    def shards(start_state, fine_nodes):
        length = start_state.shape[1]
        total = length * n_s
        vmem = pl.BlockSpec(memory_space=pltpu.VMEM)
        dma = pltpu.SemaphoreType.DMA
        lanes = math.gcd(length, 128)
        pieces = length // lanes
        results = [
            jax.ShapeDtypeStruct((count * pieces, lanes), jnp.float32) for count in (9, 9, 3, 3)
        ]
        made = pl.pallas_call(
            functools.partial(kernel, n_t, n_s),
            out_shape=tuple(results),
            in_specs=[vmem, vmem],
            out_specs=(vmem, vmem, vmem, vmem),
            scratch_shapes=[
                pltpu.VMEM((n_s, 18 * pieces, lanes), jnp.float32),
                pltpu.VMEM((n_s, 6 * pieces, lanes), jnp.float32),
                pltpu.VMEM((3, 40, length), jnp.float32),
                pltpu.VMEM((n_t, n_s, 6 * pieces, lanes), jnp.float32),
                pltpu.VMEM((n_t + 1, n_s, 6, length), jnp.float32),
                pltpu.VMEM((n_t, n_s, 6, length), jnp.float32),
                pltpu.VMEM((n_s, 6 * pieces, lanes), jnp.float32),
                pltpu.VMEM((2, 6 * pieces, lanes), jnp.float32),
                pltpu.VMEM((total, total // CLUSTER), jnp.bfloat16),
                pltpu.VMEM((3, 32, length), jnp.bfloat16),
                dma((n_s,)), dma((n_s,)),
                dma((n_s,)), dma((n_s,)),
                dma((n_t, n_s)), dma((n_t, n_s)),
                dma((n_s,)), dma((n_s,)),
                dma, dma,
            ],
            compiler_params=pltpu.CompilerParams(collective_id=0, has_side_effects=True),
        )(start_state, fine_nodes.reshape(-1, lanes))
        made = pl.pallas_call(
            pass_on, out_shape=tuple(results), in_specs=[vmem] * 4, out_specs=(vmem,) * 4
        )(*made)
        nodes, ends = (1, 3, 3, length), (1, 3, length)
        return tuple(
            one.reshape(shape) for one, shape in zip(made, (nodes, nodes, ends, ends))
        )

    return jax.shard_map(
        shards,
        mesh=mesh,
        in_specs=(P(None, "space"), P("tm", None, None, "space")),
        out_specs=(
            P("tm", None, None, "space"),
            P("tm", None, None, "space"),
            P("tm", None, "space"),
            P("tm", None, "space"),
        ),
        check_vma=False,
    )
```

```python
import functools
import math

import jax
import jax.numpy as jnp
from jax import lax
from jax.experimental import pallas as pl
from jax.experimental.pallas import tpu as pltpu
from jax.sharding import PartitionSpec as P

CLUSTER = 16

core_squared = 0.01
step_length = 0.02


def rounded(value):
    return value.astype(jnp.bfloat16).astype(jnp.float32)


def split_three(value):
    one = rounded(value)
    two = rounded(value - one)
    return one, two, rounded(value - one - two)


def split_two(value):
    high = value.astype(jnp.bfloat16)
    return high, (value - high.astype(jnp.float32)).astype(jnp.bfloat16)


def product(left, right):
    return jnp.dot(left, right, preferred_element_type=jnp.float32)


def cross(left, right):
    return [
        left[1] * right[2] - left[2] * right[1],
        left[2] * right[0] - left[0] * right[2],
        left[0] * right[1] - left[1] * right[0],
    ]


def place_parts(state, extra):
    high = [rounded(one) for one in state[0:3]]
    low = [rounded(one - top) for one, top in zip(state[0:3], high)]
    used = [top + rest for top, rest in zip(high, low)]
    norm = used[0] * used[0] + used[1] * used[1] + used[2] * used[2] + extra
    return high, low, split_three(norm)


SOURCE_ROWS = 56
TARGET_ROWS = 16
SUM_ROWS = 32


def write_rows(ref, first, values, tiles):
    for index, value in enumerate(values):
        ref[(first + index) * tiles : (first + index + 1) * tiles, :] = value


def read_rows(ref, first, count, tiles):
    if tiles == 1:
        return ref[first : first + count, :]
    return jnp.concatenate(
        [ref[pl.ds(first * tiles + tile, count, stride=tiles), :] for tile in range(tiles)], axis=1
    )


def constant_rows(ref, first, count, value, tiles):
    shape = (count * tiles, ref.shape[1])
    ref[first * tiles : (first + count) * tiles, :] = jnp.full(shape, value, jnp.float32)


def prepare_source(ref, tiles):
    constant_rows(ref, 9, 3, 1.0, tiles)
    constant_rows(ref, 12, 4, 0.0, tiles)
    constant_rows(ref, 22, 10, 0.0, tiles)


def prepare_target(ref, tiles):
    constant_rows(ref, 6, 3, 1.0, tiles)
    constant_rows(ref, 12, 4, 0.0, tiles)


def source_operands(ref, state, tiles):
    high, low, norm = place_parts(state, 0.0)
    base = state[3:6] + cross(state[0:3], state[3:6])
    write_rows(ref, 0, high + high + list(norm), tiles)
    write_rows(ref, 16, low + low, tiles)
    write_rows(ref, 32, base, tiles)
    for axis in range(3):
        write_rows(ref, 38 + 6 * axis, [state[axis] * one for one in base], tiles)
    places = read_rows(ref, 0, 32, tiles).astype(jnp.bfloat16)
    moments = read_rows(ref, 32, 24, tiles)
    high = rounded(moments)
    low = moments - high
    for_q = jnp.concatenate([high[0:8], low[0:8]], axis=0).astype(jnp.bfloat16)
    for_h = jnp.concatenate([high, low], axis=0).astype(jnp.bfloat16)
    return places, for_q, for_h


def target_operand(ref, state, tiles):
    high, low, norm = place_parts(state, core_squared)
    write_rows(ref, 0, [-2.0 * one for one in high] + [-2.0 * one for one in low], tiles)
    write_rows(ref, 9, norm, tiles)
    half = read_rows(ref, 0, TARGET_ROWS, tiles).astype(jnp.bfloat16)
    return jnp.concatenate([half, half], axis=0)


def pair_sums(places, for_q, for_h, target, both=True):
    length = places.shape[1]
    piece = math.gcd(length, 256)
    parts_q, parts_h = [], []
    left_q, left_h = [], []
    for begin in range(0, length, piece):
        part = slice(begin, begin + piece)
        spread = lax.dot_general(
            places[:, part], target, (((0,), (0,)), ((), ())), preferred_element_type=jnp.float32
        )
        inverse = lax.rsqrt(spread)
        square = inverse * inverse
        factor = square * inverse
        steep = factor * square
        if both:
            parts_q.extend(split_two(factor))
            parts_h.extend(split_two(steep))
            left_q.extend([for_q[:, part]] * 2)
            left_h.extend([for_h[:, part]] * 2)
        else:
            parts_q.append(factor.astype(jnp.bfloat16))
            parts_h.append(steep.astype(jnp.bfloat16))
            left_q.append(for_q[:, part])
            left_h.append(for_h[:, part])

    def total(left, right):
        return product(jnp.concatenate(left, axis=1), jnp.concatenate(right, axis=0))

    got_q = total(left_q, parts_q)
    got_h = total(left_h, parts_h)
    return jnp.concatenate([got_q[0:8] + got_q[8:16], got_h[0:24] + got_h[24:48]], axis=0)


def put_sums(ref, sums, first, tiles):
    lanes = ref.shape[1]
    for tile in range(sums.shape[1] // lanes):
        ref[pl.ds(first + tile, SUM_ROWS, stride=tiles), :] = sums[:, tile * lanes : (tile + 1) * lanes]


def finish(ref, state, coupling, tiles):
    def row(index):
        return ref[index * tiles : (index + 1) * tiles, :]

    places, strengths = state[0:3], state[3:6]
    weighted = [row(index) for index in range(3)]
    turned = cross(places, weighted)
    velocity = [turned[index] - row(3 + index) for index in range(3)]
    along = strengths[0] * places[0] + strengths[1] * places[1] + strengths[2] * places[2]
    moment = [
        3.0
        * (
            along * row(8 + index)
            - strengths[0] * row(14 + index)
            - strengths[1] * row(20 + index)
            - strengths[2] * row(26 + index)
        )
        for index in range(6)
    ]
    bent = cross(places, moment[0:3])
    straight = cross(strengths, weighted)
    stretch = [straight[index] - (bent[index] - moment[3 + index]) for index in range(3)]
    return [-coupling * one for one in velocity + stretch]


def kernel(
    n_t,
    n_s,
    start_ref,
    nodes_ref,
    places_out,
    strengths_out,
    next_places_out,
    next_strengths_out,
    gathered,
    begin,
    sums,
    steps,
    history,
    coarse,
    middles,
    handed,
    pool,
    merged,
    sources,
    targets,
    totals,
    many_source,
    many_target,
    many_total,
    send_a,
    recv_a,
    send_b,
    recv_b,
    send_e,
    recv_e,
    send_w,
    recv_w,
    send_h,
    recv_h,
):
    length = start_ref.shape[1]
    coupling = 1.0 / (4.0 * math.pi * math.sqrt(length * n_s))
    mine = lax.axis_index("tm")
    me = lax.axis_index("space")
    lanes = nodes_ref.shape[1]
    pieces = length // lanes
    rows = 6 * pieces
    tiles = n_s * pieces
    total = n_s * length
    clusters = total // CLUSTER
    cluster_tiles = max(1, clusters // lanes)

    def remote(source, target, send, recv, device):
        return pltpu.make_async_remote_copy(
            src_ref=source, dst_ref=target, send_sem=send, recv_sem=recv,
            device_id=device, device_id_type=pl.DeviceIdType.MESH,
        )

    def comps(ref, base=0):
        return [ref[base + one * pieces : base + (one + 1) * pieces, :] for one in range(6)]

    def flat(ref, base=0):
        return jnp.concatenate(
            [ref[pl.ds(base + piece, 6, stride=pieces), :] for piece in range(pieces)], axis=1
        )

    def near(rank):
        left, right = me, n_s - 1 - me
        both_sides = jnp.minimum(left, right)
        inner = rank <= 2 * both_sides
        distance = jnp.where(inner, (rank + 1) // 2, rank - both_sides)
        leftward = jnp.where(inner, rank % 2 == 1, left > right)
        return jnp.where(leftward, me - distance, me + distance)

    peers = [near(rank) for rank in range(1, n_s)]

    barrier = pltpu.get_barrier_semaphore()
    for offset in range(1, n_s):
        pl.semaphore_signal(
            barrier, inc=1, device_id={"space": lax.rem(me + offset, n_s)},
            device_id_type=pl.DeviceIdType.MESH,
        )
    for turn in range(1, n_t):
        pl.semaphore_signal(
            barrier, inc=1, device_id={"tm": lax.rem(mine + turn, n_t)},
            device_id_type=pl.DeviceIdType.MESH,
        )
    for piece in range(pieces):
        begin[me, pl.ds(piece, 6, stride=pieces), :] = start_ref[:, piece * lanes : (piece + 1) * lanes]
    pl.semaphore_wait(barrier, n_s - 1 + n_t - 1)

    def node_copy(peer, slot):
        return remote(nodes_ref, gathered.at[slot], send_a.at[peer], recv_a.at[slot], {"space": peer})

    def start_copy(peer, slot):
        return remote(begin.at[me], begin.at[slot], send_b.at[peer], recv_b.at[slot], {"space": peer})

    for peer in reversed(peers):
        node_copy(peer, me).start()
    for peer in reversed(peers):
        start_copy(peer, me).start()

    particle = lax.broadcasted_iota(jnp.int32, (total, clusters), 0)
    cluster = lax.broadcasted_iota(jnp.int32, (total, clusters), 1)
    offset_in = particle - cluster * CLUSTER
    pool[...] = jnp.where((offset_in >= 0) & (offset_in < CLUSTER), 1.0, 0.0).astype(jnp.bfloat16)
    for one in range(sources.shape[0]):
        prepare_source(sources.at[one], pieces)
    for one in range(targets.shape[0]):
        prepare_target(targets.at[one], pieces)
    for one in range(many_source.shape[0]):
        prepare_source(many_source.at[one], cluster_tiles)
    prepare_target(many_target, tiles)

    def coarse_sources(blocks, slot):
        state = jnp.concatenate(blocks, axis=1)
        state = jnp.concatenate([state, jnp.zeros((2, state.shape[1]), state.dtype)], axis=0)
        parts = jnp.concatenate(split_three(state), axis=0).astype(jnp.bfloat16)
        got = product(parts, pool[...])
        whole = got[0:8] + got[8:16] + got[16:24]
        if cluster_tiles == 1:
            merged[slot] = whole
        else:
            for tile in range(cluster_tiles):
                merged[slot, pl.ds(tile, 8, stride=cluster_tiles), :] = whole[
                    :, tile * lanes : (tile + 1) * lanes
                ]

        def part(index):
            return merged[slot, index * cluster_tiles : (index + 1) * cluster_tiles, :]

        mean = [part(index) * (1.0 / CLUSTER) for index in range(3)]
        return source_operands(
            many_source.at[slot], mean + [part(index) for index in range(3, 6)], cluster_tiles
        )

    own = [comps(nodes_ref, node * rows) for node in range(3)]
    spots = [target_operand(targets.at[node], own[node], pieces) for node in range(3)]
    for rank in range(n_s):
        if rank > 0:
            source = peers[rank - 1]
            node_copy(source, source).wait_recv()
        for node in range(3):
            state = comps(gathered.at[source], node * rows) if rank > 0 else own[node]
            got = pair_sums(
                *source_operands(sources.at[rank * 3 + node], state, pieces), spots[node], node == 1
            )
            if rank == 0:
                sums[node] = got
            elif rank < n_s - 1:
                sums[node] = sums[node] + got
            else:
                put_sums(totals.at[node], sums[node] + got, 0, pieces)

    def node_blocks(node):
        return [flat(nodes_ref, node * rows)] + [flat(gathered.at[peer], node * rows) for peer in peers]

    fine = [
        finish(totals.at[node], comps(nodes_ref, node * rows), coupling, pieces) for node in range(3)
    ]

    def coarse_value(blocks, slot, spot, state, both):
        put_sums(totals.at[3 + slot], pair_sums(*coarse_sources(blocks, slot), spot, both), 0, pieces)
        return finish(totals.at[3 + slot], state, coupling, pieces)

    coarse_first = coarse_value(node_blocks(0), 0, spots[0], comps(nodes_ref), True)
    for one in range(6):
        steps[mine, me, one * pieces : (one + 1) * pieces, :] = step_length * (
            (fine[0][one] + 4.0 * fine[1][one] + fine[2][one]) / 6.0 - coarse_first[one]
        )

    def step_copy(turn, peer, slice_in, place_in):
        return remote(
            steps.at[slice_in, place_in], steps.at[slice_in, place_in],
            send_e.at[turn, peer], recv_e.at[slice_in, place_in], {"tm": turn, "space": peer},
        )

    def hand_out():
        def to_slice(count, carry):
            turn = n_t - 1 - count
            for peer in peers:
                step_copy(turn, peer, mine, me).start()
            step_copy(turn, me, mine, me).start()
            return carry

        lax.fori_loop(0, n_t - 1 - mine, to_slice, 0)
        for peer in peers:
            step_copy(mine, peer, mine, me).start()

    early = n_t // 4

    @pl.when(mine < early)
    def _():
        hand_out()

    def spread_state(step):
        return [history[step, one * tiles : (one + 1) * tiles, :] for one in range(6)]

    def history_blocks(step):
        return [
            jnp.concatenate(
                [history[step, pl.ds(tile, 6, stride=tiles), :] for tile in range(tiles)], axis=1
            )
        ]

    def coarse_step(step):
        operands = coarse_sources(history_blocks(step), 2)
        state = spread_state(step)
        spot = target_operand(many_target, state, tiles)
        for z in range(n_s):
            got = pair_sums(*operands, spot[:, z * length : (z + 1) * length])
            put_sums(many_total, got, z * pieces, tiles)
        value = finish(many_total, state, coupling, tiles)
        for one in range(6):
            coarse[step, one * tiles : (one + 1) * tiles, :] = value[one]

    def advance(step):
        for one in range(6):
            for z in range(n_s):
                at = one * tiles + z * pieces
                history[step + 1, at : at + pieces, :] = (
                    history[step, at : at + pieces, :]
                    + step_length * coarse[step, at : at + pieces, :]
                    + steps[step, z, one * pieces : (one + 1) * pieces, :]
                )

    def block(ref, step, place):
        return [
            ref[step, pl.ds(one * tiles + place * pieces, pieces), :] for one in range(6)
        ]

    for peer in peers:
        start_copy(peer, peer).wait_recv()
    for z in range(n_s):
        for one in range(6):
            at = one * tiles + z * pieces
            history[0, at : at + pieces, :] = begin[z, one * pieces : (one + 1) * pieces, :]
    coarse_last = coarse_value(node_blocks(2), 1, spots[2], comps(nodes_ref, 2 * rows), False)

    @pl.when(mine >= early)
    def _():
        hand_out()

    coarse_step(0)

    def chain_step(step, carry):
        for z in range(n_s):
            step_copy(mine, me, step, z).wait_recv()
        advance(step)
        coarse_step(step + 1)
        return carry

    lax.fori_loop(0, mine, chain_step, 0)
    for peer in peers:
        step_copy(mine, me, mine, peer).wait_recv()
    advance(mine)

    initial = block(history, mine, me)
    final_state = block(history, mine + 1, me)
    spot = target_operand(targets.at[3], final_state, pieces)
    coarse_end = coarse_value(history_blocks(mine + 1), 3, spot, final_state, False)
    first = block(coarse, mine, me)
    change_first = [first[one] - coarse_first[one] for one in range(6)]
    change_last = [coarse_end[one] - coarse_last[one] for one in range(6)]
    fixed_first = [fine[0][one] + change_first[one] for one in range(6)]
    fixed_middle = [fine[1][one] + 0.5 * (change_first[one] + change_last[one]) for one in range(6)]
    fixed_last = [fine[2][one] + change_last[one] for one in range(6)]

    spot = target_operand(targets.at[4], initial, pieces)
    got = None
    for z in range(n_s):
        state = [history[mine, one * tiles + z * pieces : one * tiles + (z + 1) * pieces, :] for one in range(6)]
        more = pair_sums(*source_operands(sources.at[z], state, pieces), spot, False)
        got = more if got is None else got + more
    put_sums(totals.at[0], got, 0, pieces)
    slope_first = finish(totals.at[0], initial, coupling, pieces)
    sweep_middle = [
        initial[one]
        + 0.5 * step_length * (slope_first[one] - fixed_first[one])
        + step_length * (5.0 * fixed_first[one] + 8.0 * fixed_middle[one] - fixed_last[one]) / 24.0
        for one in range(6)
    ]
    for one in range(6):
        middles[me, one * pieces : (one + 1) * pieces, :] = sweep_middle[one]

    def middle_copy(peer, slot):
        return remote(middles.at[me], middles.at[slot], send_w.at[peer], recv_w.at[slot], {"space": peer})

    for peer in reversed(peers):
        middle_copy(peer, me).start()
    half = 3 * pieces

    def write_out(node, state):
        for one in range(3):
            at = node * half + one * pieces
            places_out[at : at + pieces, :] = state[one]
            strengths_out[at : at + pieces, :] = state[3 + one]

    write_out(0, initial)
    write_out(1, sweep_middle)
    spot = target_operand(targets.at[5], sweep_middle, pieces)
    sums[1] = pair_sums(*source_operands(sources.at[n_s], sweep_middle, pieces), spot, False)
    for rank, peer in enumerate(peers):
        middle_copy(peer, peer).wait_recv()
        got = pair_sums(
            *source_operands(sources.at[n_s + 1 + rank], comps(middles.at[peer]), pieces), spot, False
        )
        if rank < n_s - 2:
            sums[1] = sums[1] + got
        else:
            put_sums(totals.at[1], sums[1] + got, 0, pieces)
    slope_middle = finish(totals.at[1], sweep_middle, coupling, pieces)
    sweep_last = [
        sweep_middle[one]
        + 0.5 * step_length * (slope_middle[one] - fixed_middle[one])
        + step_length * (-fixed_first[one] + 8.0 * fixed_middle[one] + 5.0 * fixed_last[one]) / 24.0
        for one in range(6)
    ]
    for one in range(6):
        handed[0, one * pieces : (one + 1) * pieces, :] = sweep_last[one]

    def last_copy():
        return remote(handed.at[0], handed.at[1], send_h, recv_h, {"tm": lax.rem(mine + 1, n_t)})

    @pl.when(mine < n_t - 1)
    def _():
        last_copy().start()

    write_out(2, sweep_last)
    for peer in peers:
        node_copy(peer, me).wait_send()
        start_copy(peer, me).wait_send()
        middle_copy(peer, me).wait_send()
        step_copy(mine, peer, mine, me).wait_send()

    def sent(turn, carry):
        for peer in range(n_s):
            step_copy(turn, peer, mine, me).wait_send()
        return carry

    lax.fori_loop(mine + 1, n_t, sent, 0)

    @pl.when(mine == 0)
    def _():
        next_places_out[...] = begin[me, 0:half, :]
        next_strengths_out[...] = begin[me, half : 2 * half, :]

    @pl.when(mine > 0)
    def _():
        last_copy().wait_recv()
        next_places_out[...] = handed[1, 0:half]
        next_strengths_out[...] = handed[1, half : 2 * half]

    @pl.when(mine < n_t - 1)
    def _():
        last_copy().wait_send()


def pass_on(*refs):
    count = len(refs) // 2
    for source, target in zip(refs[:count], refs[count:]):
        size = target.shape[1]
        for one in range(target.shape[0]):
            target[one] = source[one * size : (one + 1) * size, :]


def solution(mesh):
    n_t, n_s = mesh.shape["tm"], mesh.shape["space"]

    def shards(start_state, fine_nodes):
        length = start_state.shape[1]
        total = length * n_s
        vmem = pl.BlockSpec(memory_space=pltpu.VMEM)
        dma = pltpu.SemaphoreType.DMA
        lanes = math.gcd(length, 128)
        pieces = length // lanes
        tiles = n_s * pieces
        clusters = total // CLUSTER
        cluster_tiles = max(1, clusters // lanes)
        wide = min(clusters, lanes)

        def scratch(*shape):
            return pltpu.VMEM(shape, jnp.float32)

        made = pl.pallas_call(
            functools.partial(kernel, n_t, n_s),
            out_shape=tuple(
                jax.ShapeDtypeStruct((count * pieces, lanes), jnp.float32) for count in (9, 9, 3, 3)
            ),
            in_specs=[vmem, vmem],
            out_specs=(vmem, vmem, vmem, vmem),
            scratch_shapes=[
                scratch(n_s, 18 * pieces, lanes),
                scratch(n_s, 6 * pieces, lanes),
                scratch(3, SUM_ROWS, length),
                scratch(n_t, n_s, 6 * pieces, lanes),
                scratch(n_t + 1, 6 * tiles, lanes),
                scratch(n_t, 6 * tiles, lanes),
                scratch(n_s, 6 * pieces, lanes),
                scratch(2, 6 * pieces, lanes),
                pltpu.VMEM((total, clusters), jnp.bfloat16),
                scratch(4, 8 * cluster_tiles, wide),
                scratch(3 * n_s, SOURCE_ROWS * pieces, lanes),
                scratch(6, TARGET_ROWS * pieces, lanes),
                scratch(7, SUM_ROWS * pieces, lanes),
                scratch(4, SOURCE_ROWS * cluster_tiles, wide),
                scratch(TARGET_ROWS * tiles, lanes),
                scratch(SUM_ROWS * tiles, lanes),
                dma((n_s,)), dma((n_s,)),
                dma((n_s,)), dma((n_s,)),
                dma((n_t, n_s)), dma((n_t, n_s)),
                dma((n_s,)), dma((n_s,)),
                dma, dma,
            ],
            compiler_params=pltpu.CompilerParams(collective_id=0, has_side_effects=True),
        )(start_state, fine_nodes.reshape(-1, lanes))
        made = pl.pallas_call(
            pass_on,
            out_shape=tuple(
                jax.ShapeDtypeStruct((count, pieces, lanes), jnp.float32) for count in (9, 9, 3, 3)
            ),
            in_specs=[vmem] * 4,
            out_specs=(vmem,) * 4,
        )(*made)
        nodes, ends = (1, 3, 3, length), (1, 3, length)
        return tuple(
            one.reshape(shape) for one, shape in zip(made, (nodes, nodes, ends, ends))
        )

    return jax.shard_map(
        shards,
        mesh=mesh,
        in_specs=(P(None, "space"), P("tm", None, None, "space")),
        out_specs=(
            P("tm", None, None, "space"),
            P("tm", None, None, "space"),
            P("tm", None, "space"),
            P("tm", None, "space"),
        ),
        check_vma=False,
    )
```

```python
import functools
import math

import jax
import jax.numpy as jnp
from jax import lax
from jax.experimental import pallas as pl
from jax.experimental.pallas import tpu as pltpu
from jax.sharding import PartitionSpec as P

CLUSTER = 16

core_squared = 0.01
step_length = 0.02


def rounded(value):
    return value.astype(jnp.bfloat16).astype(jnp.float32)


def split_three(value):
    one = rounded(value)
    two = rounded(value - one)
    return one, two, rounded(value - one - two)


def split_two(value):
    high = value.astype(jnp.bfloat16)
    return high, (value - high.astype(jnp.float32)).astype(jnp.bfloat16)


def product(left, right):
    return jnp.dot(left, right, preferred_element_type=jnp.float32)


def cross(left, right):
    return [
        left[1] * right[2] - left[2] * right[1],
        left[2] * right[0] - left[0] * right[2],
        left[0] * right[1] - left[1] * right[0],
    ]


def place_parts(state, extra):
    high = [rounded(one) for one in state[0:3]]
    low = [rounded(one - top) for one, top in zip(state[0:3], high)]
    used = [top + rest for top, rest in zip(high, low)]
    norm = used[0] * used[0] + used[1] * used[1] + used[2] * used[2] + extra
    return high, low, split_three(norm)


SOURCE_ROWS = 56
TARGET_ROWS = 16
SUM_ROWS = 32


def write_rows(ref, first, values, tiles):
    for index, value in enumerate(values):
        ref[(first + index) * tiles : (first + index + 1) * tiles, :] = value


def read_rows(ref, first, count, tiles):
    if tiles == 1:
        return ref[first : first + count, :]
    return jnp.concatenate(
        [ref[pl.ds(first * tiles + tile, count, stride=tiles), :] for tile in range(tiles)], axis=1
    )


def constant_rows(ref, first, count, value, tiles):
    shape = (count * tiles, ref.shape[1])
    ref[first * tiles : (first + count) * tiles, :] = jnp.full(shape, value, jnp.float32)


def prepare_source(ref, tiles):
    constant_rows(ref, 9, 3, 1.0, tiles)
    constant_rows(ref, 12, 4, 0.0, tiles)
    constant_rows(ref, 22, 10, 0.0, tiles)


def prepare_target(ref, tiles):
    constant_rows(ref, 6, 3, 1.0, tiles)
    constant_rows(ref, 12, 4, 0.0, tiles)


def source_operands(ref, state, tiles):
    high, low, norm = place_parts(state, 0.0)
    base = state[3:6] + cross(state[0:3], state[3:6])
    write_rows(ref, 0, high + high + list(norm), tiles)
    write_rows(ref, 16, low + low, tiles)
    write_rows(ref, 32, base, tiles)
    for axis in range(3):
        write_rows(ref, 38 + 6 * axis, [state[axis] * one for one in base], tiles)
    places = read_rows(ref, 0, 32, tiles).astype(jnp.bfloat16)
    moments = read_rows(ref, 32, 24, tiles)
    high = rounded(moments)
    low = moments - high
    for_q = jnp.concatenate([high[0:8], low[0:8]], axis=0).astype(jnp.bfloat16)
    for_h = jnp.concatenate([high, low], axis=0).astype(jnp.bfloat16)
    return places, for_q, for_h


def target_operand(ref, state, tiles):
    high, low, norm = place_parts(state, core_squared)
    write_rows(ref, 0, [-2.0 * one for one in high] + [-2.0 * one for one in low], tiles)
    write_rows(ref, 9, norm, tiles)
    half = read_rows(ref, 0, TARGET_ROWS, tiles).astype(jnp.bfloat16)
    return jnp.concatenate([half, half], axis=0)


def spread_of(job):
    return lax.dot_general(
        job[0], job[3], (((0,), (0,)), ((), ())), preferred_element_type=jnp.float32
    )


def factors_of(job, spread):
    inverse = lax.rsqrt(spread)
    square = inverse * inverse
    factor = square * inverse
    steep = factor * square
    if job[4]:
        return (
            jnp.concatenate(split_two(factor), axis=0),
            jnp.concatenate(split_two(steep), axis=0),
        )
    return factor.astype(jnp.bfloat16), steep.astype(jnp.bfloat16)


def sums_of(job, factors):
    for_q, for_h = job[1], job[2]
    if job[4]:
        for_q = jnp.concatenate([for_q, for_q], axis=1)
        for_h = jnp.concatenate([for_h, for_h], axis=1)
    got_q = product(for_q, factors[0])
    got_h = product(for_h, factors[1])
    return jnp.concatenate([got_q[0:8] + got_q[8:16], got_h[0:24] + got_h[24:48]], axis=0)


def cut(operands, target, both):
    places, for_q, for_h = operands
    length = places.shape[1]
    piece = math.gcd(length, 256)
    return [
        (places[:, at : at + piece], for_q[:, at : at + piece], for_h[:, at : at + piece], target, both)
        for at in range(0, length, piece)
    ]


def run(groups):
    jobs = [job for group in groups for job in group]
    spreads, factors, sums = {}, {}, {}
    for turn in range(len(jobs) + 2):
        if turn < len(jobs):
            spreads[turn] = spread_of(jobs[turn])
        if 0 <= turn - 2:
            sums[turn - 2] = sums_of(jobs[turn - 2], factors.pop(turn - 2))
        if 0 <= turn - 1 < len(jobs):
            factors[turn - 1] = factors_of(jobs[turn - 1], spreads.pop(turn - 1))
    results, at = [], 0
    for group in groups:
        total = sums[at]
        for more in range(at + 1, at + len(group)):
            total = total + sums[more]
        at += len(group)
        results.append(total)
    return results


def pair_sums(places, for_q, for_h, target, both=True):
    return run([cut((places, for_q, for_h), target, both)])[0]


def whole_sums(places, for_q, for_h, target, both=True):
    length = places.shape[1]
    piece = math.gcd(length, 256)
    parts_q, parts_h = [], []
    left_q, left_h = [], []
    for begin in range(0, length, piece):
        part = slice(begin, begin + piece)
        spread = lax.dot_general(
            places[:, part], target, (((0,), (0,)), ((), ())), preferred_element_type=jnp.float32
        )
        inverse = lax.rsqrt(spread)
        square = inverse * inverse
        factor = square * inverse
        steep = factor * square
        if both:
            parts_q.extend(split_two(factor))
            parts_h.extend(split_two(steep))
            left_q.extend([for_q[:, part]] * 2)
            left_h.extend([for_h[:, part]] * 2)
        else:
            parts_q.append(factor.astype(jnp.bfloat16))
            parts_h.append(steep.astype(jnp.bfloat16))
            left_q.append(for_q[:, part])
            left_h.append(for_h[:, part])

    def total(left, right):
        return product(jnp.concatenate(left, axis=1), jnp.concatenate(right, axis=0))

    got_q = total(left_q, parts_q)
    got_h = total(left_h, parts_h)
    return jnp.concatenate([got_q[0:8] + got_q[8:16], got_h[0:24] + got_h[24:48]], axis=0)


def put_sums(ref, sums, first, tiles):
    lanes = ref.shape[1]
    for tile in range(sums.shape[1] // lanes):
        ref[pl.ds(first + tile, SUM_ROWS, stride=tiles), :] = sums[:, tile * lanes : (tile + 1) * lanes]


def finish(ref, state, coupling, tiles):
    def row(index):
        return ref[index * tiles : (index + 1) * tiles, :]

    places, strengths = state[0:3], state[3:6]
    weighted = [row(index) for index in range(3)]
    turned = cross(places, weighted)
    velocity = [turned[index] - row(3 + index) for index in range(3)]
    along = strengths[0] * places[0] + strengths[1] * places[1] + strengths[2] * places[2]
    moment = [
        3.0
        * (
            along * row(8 + index)
            - strengths[0] * row(14 + index)
            - strengths[1] * row(20 + index)
            - strengths[2] * row(26 + index)
        )
        for index in range(6)
    ]
    bent = cross(places, moment[0:3])
    straight = cross(strengths, weighted)
    stretch = [straight[index] - (bent[index] - moment[3 + index]) for index in range(3)]
    return [-coupling * one for one in velocity + stretch]


def kernel(
    n_t,
    n_s,
    start_ref,
    nodes_ref,
    places_out,
    strengths_out,
    next_places_out,
    next_strengths_out,
    gathered,
    begin,
    sums,
    steps,
    history,
    coarse,
    middles,
    handed,
    pool,
    merged,
    sources,
    targets,
    totals,
    many_source,
    many_target,
    many_total,
    send_a,
    recv_a,
    send_b,
    recv_b,
    send_e,
    recv_e,
    send_w,
    recv_w,
    send_h,
    recv_h,
):
    length = start_ref.shape[1]
    coupling = 1.0 / (4.0 * math.pi * math.sqrt(length * n_s))
    mine = lax.axis_index("tm")
    me = lax.axis_index("space")
    lanes = nodes_ref.shape[1]
    pieces = length // lanes
    rows = 6 * pieces
    tiles = n_s * pieces
    total = n_s * length
    clusters = total // CLUSTER
    cluster_tiles = max(1, clusters // lanes)

    def remote(source, target, send, recv, device):
        return pltpu.make_async_remote_copy(
            src_ref=source, dst_ref=target, send_sem=send, recv_sem=recv,
            device_id=device, device_id_type=pl.DeviceIdType.MESH,
        )

    def comps(ref, base=0):
        return [ref[base + one * pieces : base + (one + 1) * pieces, :] for one in range(6)]

    def near(rank):
        left, right = me, n_s - 1 - me
        both_sides = jnp.minimum(left, right)
        inner = rank <= 2 * both_sides
        distance = jnp.where(inner, (rank + 1) // 2, rank - both_sides)
        leftward = jnp.where(inner, rank % 2 == 1, left > right)
        return jnp.where(leftward, me - distance, me + distance)

    peers = [near(rank) for rank in range(1, n_s)]

    barrier = pltpu.get_barrier_semaphore()
    for offset in range(1, n_s):
        pl.semaphore_signal(
            barrier, inc=1, device_id={"space": lax.rem(me + offset, n_s)},
            device_id_type=pl.DeviceIdType.MESH,
        )
    for turn in range(1, n_t):
        pl.semaphore_signal(
            barrier, inc=1, device_id={"tm": lax.rem(mine + turn, n_t)},
            device_id_type=pl.DeviceIdType.MESH,
        )
    for piece in range(pieces):
        begin[me, pl.ds(piece, 6, stride=pieces), :] = start_ref[:, piece * lanes : (piece + 1) * lanes]
    pl.semaphore_wait(barrier, n_s - 1 + n_t - 1)

    def node_copy(peer, slot):
        return remote(nodes_ref, gathered.at[slot], send_a.at[peer], recv_a.at[slot], {"space": peer})

    def start_copy(peer, slot):
        return remote(begin.at[me], begin.at[slot], send_b.at[peer], recv_b.at[slot], {"space": peer})

    for peer in reversed(peers):
        node_copy(peer, me).start()
    for peer in reversed(peers):
        start_copy(peer, me).start()

    per_tile = lanes // CLUSTER
    inside = lax.broadcasted_iota(jnp.int32, (lanes, lanes), 0) // CLUSTER
    wanted = lax.broadcasted_iota(jnp.int32, (lanes, lanes), 1) % per_tile
    pool[...] = jnp.where(inside == wanted, 1.0, 0.0).astype(jnp.bfloat16)
    tile_of = lax.broadcasted_iota(jnp.int32, (CLUSTER, lanes), 0)
    owner = lax.broadcasted_iota(jnp.int32, (CLUSTER, lanes), 1) // per_tile
    merged[...] = jnp.where(tile_of == owner, 1.0, 0.0)
    for one in range(sources.shape[0]):
        prepare_source(sources.at[one], pieces)
    for one in range(targets.shape[0]):
        prepare_target(targets.at[one], pieces)
    for one in range(many_source.shape[0]):
        prepare_source(many_source.at[one], cluster_tiles)
    prepare_target(many_target, tiles)

    def coarse_sources(blocks, slot):
        count = blocks[0].shape[0] // 6
        parts = [part for block in blocks for part in split_three(block)]
        got = product(jnp.concatenate(parts, axis=0).astype(jnp.bfloat16), pool[...])
        size = 6 * count
        sums = []
        for at in range(0, got.shape[0], 3 * size):
            sums.append(got[at : at + size] + got[at + size : at + 2 * size] + got[at + 2 * size : at + 3 * size])
        state = []
        for one in range(6):
            tops = []
            for first in range(0, tiles, CLUSTER):
                total_of = None
                for tile in range(first, min(first + CLUSTER, tiles), min(count, CLUSTER)):
                    block, inner = sums[tile // count], tile % count
                    width = min(count, CLUSTER)
                    shift = tile - first
                    kept = (
                        block[one * count + inner : one * count + inner + width]
                        * merged[shift : shift + width, :]
                    )
                    kept = jnp.sum(kept, axis=0, keepdims=True)
                    total_of = kept if total_of is None else total_of + kept
                tops.append(total_of)
            whole = tops[0] if len(tops) == 1 else jnp.concatenate(tops, axis=0)
            state.append(whole * (1.0 / CLUSTER) if one < 3 else whole)
        return source_operands(many_source.at[slot], state, cluster_tiles)

    own = [comps(nodes_ref, node * rows) for node in range(3)]
    spots = [target_operand(targets.at[node], own[node], pieces) for node in range(3)]
    for rank in range(n_s):
        if rank > 0:
            source = peers[rank - 1]
            node_copy(source, source).wait_recv()
        for node in range(3):
            state = comps(gathered.at[source], node * rows) if rank > 0 else own[node]
            got = whole_sums(
                *source_operands(sources.at[rank * 3 + node], state, pieces), spots[node], node == 1
            )
            if rank == 0:
                sums[node] = got
            elif rank < n_s - 1:
                sums[node] = sums[node] + got
            else:
                put_sums(totals.at[node], sums[node] + got, 0, pieces)

    def node_blocks(node):
        part = pl.ds(node * rows, rows)
        return [nodes_ref[part, :]] + [gathered[peer, part, :] for peer in peers]

    fine = [
        finish(totals.at[node], comps(nodes_ref, node * rows), coupling, pieces) for node in range(3)
    ]

    def coarse_value(blocks, slot, spot, state, both):
        put_sums(totals.at[3 + slot], pair_sums(*coarse_sources(blocks, slot), spot, both), 0, pieces)
        return finish(totals.at[3 + slot], state, coupling, pieces)

    coarse_first = coarse_value(node_blocks(0), 0, spots[0], comps(nodes_ref), True)
    for one in range(6):
        steps[mine, me, one * pieces : (one + 1) * pieces, :] = step_length * (
            (fine[0][one] + 4.0 * fine[1][one] + fine[2][one]) / 6.0 - coarse_first[one]
        )

    def step_copy(turn, peer, slice_in, place_in):
        return remote(
            steps.at[slice_in, place_in], steps.at[slice_in, place_in],
            send_e.at[turn, peer], recv_e.at[slice_in, place_in], {"tm": turn, "space": peer},
        )

    def hand_out():
        def to_slice(count, carry):
            turn = n_t - 1 - count
            for peer in peers:
                step_copy(turn, peer, mine, me).start()
            step_copy(turn, me, mine, me).start()
            return carry

        lax.fori_loop(0, n_t - 1 - mine, to_slice, 0)
        for peer in peers:
            step_copy(mine, peer, mine, me).start()

    early = n_t // 4

    @pl.when(mine < early)
    def _():
        hand_out()

    def spread_state(step):
        return [history[step, one * tiles : (one + 1) * tiles, :] for one in range(6)]

    def history_blocks(step):
        return [history[step]]

    def coarse_step(step):
        operands = coarse_sources(history_blocks(step), 2)
        state = spread_state(step)
        spot = target_operand(many_target, state, tiles)
        groups = [
            cut(operands, spot[:, z * length : (z + 1) * length], True) for z in range(n_s)
        ]
        for z, got in enumerate(run(groups)):
            put_sums(many_total, got, z * pieces, tiles)
        value = finish(many_total, state, coupling, tiles)
        for one in range(6):
            coarse[step, one * tiles : (one + 1) * tiles, :] = value[one]

    def advance(step):
        for one in range(6):
            for z in range(n_s):
                at = one * tiles + z * pieces
                history[step + 1, at : at + pieces, :] = (
                    history[step, at : at + pieces, :]
                    + step_length * coarse[step, at : at + pieces, :]
                    + steps[step, z, one * pieces : (one + 1) * pieces, :]
                )

    def block(ref, step, place):
        return [
            ref[step, pl.ds(one * tiles + place * pieces, pieces), :] for one in range(6)
        ]

    for peer in peers:
        start_copy(peer, peer).wait_recv()
    for z in range(n_s):
        for one in range(6):
            at = one * tiles + z * pieces
            history[0, at : at + pieces, :] = begin[z, one * pieces : (one + 1) * pieces, :]
    coarse_last = coarse_value(node_blocks(2), 1, spots[2], comps(nodes_ref, 2 * rows), False)

    @pl.when(mine >= early)
    def _():
        hand_out()

    coarse_step(0)

    def chain_step(step, carry):
        for z in range(n_s):
            step_copy(mine, me, step, z).wait_recv()
        advance(step)
        coarse_step(step + 1)
        return carry

    lax.fori_loop(0, mine, chain_step, 0)
    for peer in peers:
        step_copy(mine, me, mine, peer).wait_recv()
    advance(mine)

    initial = block(history, mine, me)
    final_state = block(history, mine + 1, me)
    spot = target_operand(targets.at[3], final_state, pieces)
    coarse_end = coarse_value(history_blocks(mine + 1), 3, spot, final_state, False)
    first = block(coarse, mine, me)
    change_first = [first[one] - coarse_first[one] for one in range(6)]
    change_last = [coarse_end[one] - coarse_last[one] for one in range(6)]
    fixed_first = [fine[0][one] + change_first[one] for one in range(6)]
    fixed_middle = [fine[1][one] + 0.5 * (change_first[one] + change_last[one]) for one in range(6)]
    fixed_last = [fine[2][one] + change_last[one] for one in range(6)]

    spot = target_operand(targets.at[4], initial, pieces)
    got = None
    for z in range(n_s):
        state = [history[mine, one * tiles + z * pieces : one * tiles + (z + 1) * pieces, :] for one in range(6)]
        more = whole_sums(*source_operands(sources.at[z], state, pieces), spot, False)
        got = more if got is None else got + more
    put_sums(totals.at[0], got, 0, pieces)
    slope_first = finish(totals.at[0], initial, coupling, pieces)
    sweep_middle = [
        initial[one]
        + 0.5 * step_length * (slope_first[one] - fixed_first[one])
        + step_length * (5.0 * fixed_first[one] + 8.0 * fixed_middle[one] - fixed_last[one]) / 24.0
        for one in range(6)
    ]
    for one in range(6):
        middles[me, one * pieces : (one + 1) * pieces, :] = sweep_middle[one]

    def middle_copy(peer, slot):
        return remote(middles.at[me], middles.at[slot], send_w.at[peer], recv_w.at[slot], {"space": peer})

    for peer in reversed(peers):
        middle_copy(peer, me).start()
    half = 3 * pieces

    def write_out(node, state):
        for one in range(3):
            at = node * half + one * pieces
            places_out[at : at + pieces, :] = state[one]
            strengths_out[at : at + pieces, :] = state[3 + one]

    write_out(0, initial)
    write_out(1, sweep_middle)
    spot = target_operand(targets.at[5], sweep_middle, pieces)
    sums[1] = pair_sums(*source_operands(sources.at[n_s], sweep_middle, pieces), spot, False)
    for rank, peer in enumerate(peers):
        middle_copy(peer, peer).wait_recv()
        got = pair_sums(
            *source_operands(sources.at[n_s + 1 + rank], comps(middles.at[peer]), pieces), spot, False
        )
        if rank < n_s - 2:
            sums[1] = sums[1] + got
        else:
            put_sums(totals.at[1], sums[1] + got, 0, pieces)
    slope_middle = finish(totals.at[1], sweep_middle, coupling, pieces)
    sweep_last = [
        sweep_middle[one]
        + 0.5 * step_length * (slope_middle[one] - fixed_middle[one])
        + step_length * (-fixed_first[one] + 8.0 * fixed_middle[one] + 5.0 * fixed_last[one]) / 24.0
        for one in range(6)
    ]
    for one in range(6):
        handed[0, one * pieces : (one + 1) * pieces, :] = sweep_last[one]

    def last_copy():
        return remote(handed.at[0], handed.at[1], send_h, recv_h, {"tm": lax.rem(mine + 1, n_t)})

    @pl.when(mine < n_t - 1)
    def _():
        last_copy().start()

    write_out(2, sweep_last)
    for peer in peers:
        node_copy(peer, me).wait_send()
        start_copy(peer, me).wait_send()
        middle_copy(peer, me).wait_send()
        step_copy(mine, peer, mine, me).wait_send()

    def sent(turn, carry):
        for peer in range(n_s):
            step_copy(turn, peer, mine, me).wait_send()
        return carry

    lax.fori_loop(mine + 1, n_t, sent, 0)

    @pl.when(mine == 0)
    def _():
        next_places_out[...] = begin[me, 0:half, :]
        next_strengths_out[...] = begin[me, half : 2 * half, :]

    @pl.when(mine > 0)
    def _():
        last_copy().wait_recv()
        next_places_out[...] = handed[1, 0:half]
        next_strengths_out[...] = handed[1, half : 2 * half]

    @pl.when(mine < n_t - 1)
    def _():
        last_copy().wait_send()


def pass_on(*refs):
    count = len(refs) // 2
    for source, target in zip(refs[:count], refs[count:]):
        size = target.shape[1]
        for one in range(target.shape[0]):
            target[one] = source[one * size : (one + 1) * size, :]


def solution(mesh):
    n_t, n_s = mesh.shape["tm"], mesh.shape["space"]

    def shards(start_state, fine_nodes):
        length = start_state.shape[1]
        total = length * n_s
        vmem = pl.BlockSpec(memory_space=pltpu.VMEM)
        dma = pltpu.SemaphoreType.DMA
        lanes = math.gcd(length, 128)
        pieces = length // lanes
        tiles = n_s * pieces
        clusters = total // CLUSTER
        cluster_tiles = max(1, clusters // lanes)
        wide = min(clusters, lanes)

        def scratch(*shape):
            return pltpu.VMEM(shape, jnp.float32)

        made = pl.pallas_call(
            functools.partial(kernel, n_t, n_s),
            out_shape=tuple(
                jax.ShapeDtypeStruct((count * pieces, lanes), jnp.float32) for count in (9, 9, 3, 3)
            ),
            in_specs=[vmem, vmem],
            out_specs=(vmem, vmem, vmem, vmem),
            scratch_shapes=[
                scratch(n_s, 18 * pieces, lanes),
                scratch(n_s, 6 * pieces, lanes),
                scratch(3, SUM_ROWS, length),
                scratch(n_t, n_s, 6 * pieces, lanes),
                scratch(n_t + 1, 6 * tiles, lanes),
                scratch(n_t, 6 * tiles, lanes),
                scratch(n_s, 6 * pieces, lanes),
                scratch(2, 6 * pieces, lanes),
                pltpu.VMEM((lanes, lanes), jnp.bfloat16),
                scratch(CLUSTER, lanes),
                scratch(3 * n_s, SOURCE_ROWS * pieces, lanes),
                scratch(6, TARGET_ROWS * pieces, lanes),
                scratch(7, SUM_ROWS * pieces, lanes),
                scratch(4, SOURCE_ROWS * cluster_tiles, wide),
                scratch(TARGET_ROWS * tiles, lanes),
                scratch(SUM_ROWS * tiles, lanes),
                dma((n_s,)), dma((n_s,)),
                dma((n_s,)), dma((n_s,)),
                dma((n_t, n_s)), dma((n_t, n_s)),
                dma((n_s,)), dma((n_s,)),
                dma, dma,
            ],
            compiler_params=pltpu.CompilerParams(collective_id=0, has_side_effects=True),
        )(start_state, fine_nodes.reshape(-1, lanes))
        made = pl.pallas_call(
            pass_on,
            out_shape=tuple(
                jax.ShapeDtypeStruct((count, pieces, lanes), jnp.float32) for count in (9, 9, 3, 3)
            ),
            in_specs=[vmem] * 4,
            out_specs=(vmem,) * 4,
        )(*made)
        nodes, ends = (1, 3, 3, length), (1, 3, length)
        return tuple(
            one.reshape(shape) for one, shape in zip(made, (nodes, nodes, ends, ends))
        )

    return jax.shard_map(
        shards,
        mesh=mesh,
        in_specs=(P(None, "space"), P("tm", None, None, "space")),
        out_specs=(
            P("tm", None, None, "space"),
            P("tm", None, None, "space"),
            P("tm", None, "space"),
            P("tm", None, "space"),
        ),
        check_vma=False,
    )
```

```python
import functools
import math

import jax
import jax.numpy as jnp
from jax import lax
from jax.experimental import pallas as pl
from jax.experimental.pallas import tpu as pltpu
from jax.sharding import PartitionSpec as P

CLUSTER = 16

core_squared = 0.01
step_length = 0.02


def rounded(value):
    return value.astype(jnp.bfloat16).astype(jnp.float32)


def split_three(value):
    one = rounded(value)
    two = rounded(value - one)
    return one, two, rounded(value - one - two)


def split_two(value):
    high = value.astype(jnp.bfloat16)
    return high, (value - high.astype(jnp.float32)).astype(jnp.bfloat16)


def product(left, right):
    return jnp.dot(left, right, preferred_element_type=jnp.float32)


def cross(left, right):
    return [
        left[1] * right[2] - left[2] * right[1],
        left[2] * right[0] - left[0] * right[2],
        left[0] * right[1] - left[1] * right[0],
    ]


def place_parts(state, extra):
    high = [rounded(one) for one in state[0:3]]
    low = [rounded(one - top) for one, top in zip(state[0:3], high)]
    used = [top + rest for top, rest in zip(high, low)]
    norm = used[0] * used[0] + used[1] * used[1] + used[2] * used[2] + extra
    return high, low, split_three(norm)


SLOTS = 4
SOURCE_ROWS = 56
TARGET_ROWS = 16
SUM_ROWS = 32


def write_rows(ref, first, values, tiles):
    for index, value in enumerate(values):
        ref[(first + index) * tiles : (first + index + 1) * tiles, :] = value


def read_rows(ref, first, count, tiles):
    if tiles == 1:
        return ref[first : first + count, :]
    return jnp.concatenate(
        [ref[pl.ds(first * tiles + tile, count, stride=tiles), :] for tile in range(tiles)], axis=1
    )


def constant_rows(ref, first, count, value, tiles):
    shape = (count * tiles, ref.shape[1])
    ref[first * tiles : (first + count) * tiles, :] = jnp.full(shape, value, jnp.float32)


def prepare_source(ref, tiles):
    constant_rows(ref, 9, 3, 1.0, tiles)
    constant_rows(ref, 12, 4, 0.0, tiles)
    constant_rows(ref, 22, 10, 0.0, tiles)


def prepare_target(ref, tiles):
    constant_rows(ref, 6, 3, 1.0, tiles)
    constant_rows(ref, 12, 4, 0.0, tiles)


def source_operands(ref, state, tiles):
    high, low, norm = place_parts(state, 0.0)
    base = state[3:6] + cross(state[0:3], state[3:6])
    write_rows(ref, 0, high + high + list(norm), tiles)
    write_rows(ref, 16, low + low, tiles)
    write_rows(ref, 32, base, tiles)
    for axis in range(3):
        write_rows(ref, 38 + 6 * axis, [state[axis] * one for one in base], tiles)
    places = read_rows(ref, 0, 32, tiles).astype(jnp.bfloat16)
    moments = read_rows(ref, 32, 24, tiles)
    high = rounded(moments)
    low = moments - high
    for_q = jnp.concatenate([high[0:8], low[0:8]], axis=0).astype(jnp.bfloat16)
    for_h = jnp.concatenate([high, low], axis=0).astype(jnp.bfloat16)
    return places, for_q, for_h


def target_operand(ref, state, tiles):
    high, low, norm = place_parts(state, core_squared)
    write_rows(ref, 0, [-2.0 * one for one in high] + [-2.0 * one for one in low], tiles)
    write_rows(ref, 9, norm, tiles)
    half = read_rows(ref, 0, TARGET_ROWS, tiles).astype(jnp.bfloat16)
    return jnp.concatenate([half, half], axis=0)


def spread_of(job):
    return lax.dot_general(
        job[0], job[3], (((0,), (0,)), ((), ())), preferred_element_type=jnp.float32
    )


def factors_of(job, spread):
    inverse = lax.rsqrt(spread)
    square = inverse * inverse
    factor = square * inverse
    steep = factor * square
    if job[4]:
        return (
            jnp.concatenate(split_two(factor), axis=0),
            jnp.concatenate(split_two(steep), axis=0),
        )
    return factor.astype(jnp.bfloat16), steep.astype(jnp.bfloat16)


def sums_from(job, factors):
    for_q, for_h = job[1], job[2]
    if job[4]:
        for_q = jnp.concatenate([for_q, for_q], axis=1)
        for_h = jnp.concatenate([for_h, for_h], axis=1)
    got_q = product(for_q, factors[0])
    got_h = product(for_h, factors[1])
    return jnp.concatenate([got_q[0:8] + got_q[8:16], got_h[0:24] + got_h[24:48]], axis=0)


def keep_factors(job, spread, kept, slot):
    inverse = lax.rsqrt(spread)
    square = inverse * inverse
    factor = square * inverse
    steep = factor * square
    rows = spread.shape[0]
    if job[4]:
        for part, value in ((0, factor), (2, steep)):
            high, low = split_two(value)
            kept[slot, part * rows : (part + 1) * rows, :] = high
            kept[slot, (part + 1) * rows : (part + 2) * rows, :] = low
    else:
        kept[slot, 0:rows, :] = factor.astype(jnp.bfloat16)
        kept[slot, 2 * rows : 3 * rows, :] = steep.astype(jnp.bfloat16)


def sums_of(job, kept, slot):
    for_q, for_h = job[1], job[2]
    rows = for_q.shape[1]
    if job[4]:
        for_q = jnp.concatenate([for_q, for_q], axis=1)
        for_h = jnp.concatenate([for_h, for_h], axis=1)
    got_q = product(for_q, kept[slot, 0 : for_q.shape[1], :])
    got_h = product(for_h, kept[slot, 2 * rows : 2 * rows + for_h.shape[1], :])
    return jnp.concatenate([got_q[0:8] + got_q[8:16], got_h[0:24] + got_h[24:48]], axis=0)


def cut(operands, target, both):
    places, for_q, for_h = operands
    length = places.shape[1]
    piece = math.gcd(length, 256)
    return [
        (places[:, at : at + piece], for_q[:, at : at + piece], for_h[:, at : at + piece], target, both)
        for at in range(0, length, piece)
    ]


def run(kept, groups):
    jobs = [job for group in groups for job in group]
    spreads, sums = {}, {}
    for turn in range(len(jobs) + 2):
        if turn < len(jobs):
            spreads[turn] = spread_of(jobs[turn])
        if 0 <= turn - 2:
            sums[turn - 2] = sums_of(jobs[turn - 2], kept, (turn - 2) % SLOTS)
        if 0 <= turn - 1 < len(jobs):
            keep_factors(jobs[turn - 1], spreads.pop(turn - 1), kept, (turn - 1) % SLOTS)
    results, at = [], 0
    for group in groups:
        total = sums[at]
        for more in range(at + 1, at + len(group)):
            total = total + sums[more]
        at += len(group)
        results.append(total)
    return results


def run_values(groups):
    jobs = [job for group in groups for job in group]
    spreads, factors, sums = {}, {}, {}
    for turn in range(len(jobs) + 2):
        if turn < len(jobs):
            spreads[turn] = spread_of(jobs[turn])
        if 0 <= turn - 2:
            sums[turn - 2] = sums_from(jobs[turn - 2], factors.pop(turn - 2))
        if 0 <= turn - 1 < len(jobs):
            factors[turn - 1] = factors_of(jobs[turn - 1], spreads.pop(turn - 1))
    results, at = [], 0
    for group in groups:
        total = sums[at]
        for more in range(at + 1, at + len(group)):
            total = total + sums[more]
        at += len(group)
        results.append(total)
    return results


def whole_sums(places, for_q, for_h, target, both=True):
    length = places.shape[1]
    piece = math.gcd(length, 256)
    parts_q, parts_h = [], []
    left_q, left_h = [], []
    for begin in range(0, length, piece):
        part = slice(begin, begin + piece)
        spread = lax.dot_general(
            places[:, part], target, (((0,), (0,)), ((), ())), preferred_element_type=jnp.float32
        )
        inverse = lax.rsqrt(spread)
        square = inverse * inverse
        factor = square * inverse
        steep = factor * square
        if both:
            parts_q.extend(split_two(factor))
            parts_h.extend(split_two(steep))
            left_q.extend([for_q[:, part]] * 2)
            left_h.extend([for_h[:, part]] * 2)
        else:
            parts_q.append(factor.astype(jnp.bfloat16))
            parts_h.append(steep.astype(jnp.bfloat16))
            left_q.append(for_q[:, part])
            left_h.append(for_h[:, part])

    def total(left, right):
        return product(jnp.concatenate(left, axis=1), jnp.concatenate(right, axis=0))

    got_q = total(left_q, parts_q)
    got_h = total(left_h, parts_h)
    return jnp.concatenate([got_q[0:8] + got_q[8:16], got_h[0:24] + got_h[24:48]], axis=0)


def put_sums(ref, sums, first, tiles):
    lanes = ref.shape[1]
    for tile in range(sums.shape[1] // lanes):
        ref[pl.ds(first + tile, SUM_ROWS, stride=tiles), :] = sums[:, tile * lanes : (tile + 1) * lanes]


def finish(ref, state, coupling, tiles):
    def row(index):
        return ref[index * tiles : (index + 1) * tiles, :]

    places, strengths = state[0:3], state[3:6]
    weighted = [row(index) for index in range(3)]
    turned = cross(places, weighted)
    velocity = [turned[index] - row(3 + index) for index in range(3)]
    along = strengths[0] * places[0] + strengths[1] * places[1] + strengths[2] * places[2]
    moment = [
        3.0
        * (
            along * row(8 + index)
            - strengths[0] * row(14 + index)
            - strengths[1] * row(20 + index)
            - strengths[2] * row(26 + index)
        )
        for index in range(6)
    ]
    bent = cross(places, moment[0:3])
    straight = cross(strengths, weighted)
    stretch = [straight[index] - (bent[index] - moment[3 + index]) for index in range(3)]
    return [-coupling * one for one in velocity + stretch]


def kernel(
    n_t,
    n_s,
    start_ref,
    nodes_ref,
    places_out,
    strengths_out,
    next_places_out,
    next_strengths_out,
    gathered,
    begin,
    sums,
    steps,
    history,
    coarse,
    middles,
    handed,
    pool,
    merged,
    sources,
    targets,
    totals,
    many_source,
    many_target,
    many_total,
    kept,
    send_a,
    recv_a,
    send_b,
    recv_b,
    send_e,
    recv_e,
    send_w,
    recv_w,
    send_h,
    recv_h,
):
    length = start_ref.shape[1]
    coupling = 1.0 / (4.0 * math.pi * math.sqrt(length * n_s))
    mine = lax.axis_index("tm")
    me = lax.axis_index("space")
    lanes = nodes_ref.shape[1]
    pieces = length // lanes
    rows = 6 * pieces
    tiles = n_s * pieces
    total = n_s * length
    clusters = total // CLUSTER
    cluster_tiles = max(1, clusters // lanes)

    def remote(source, target, send, recv, device):
        return pltpu.make_async_remote_copy(
            src_ref=source, dst_ref=target, send_sem=send, recv_sem=recv,
            device_id=device, device_id_type=pl.DeviceIdType.MESH,
        )

    def comps(ref, base=0):
        return [ref[base + one * pieces : base + (one + 1) * pieces, :] for one in range(6)]

    def near(rank):
        left, right = me, n_s - 1 - me
        both_sides = jnp.minimum(left, right)
        inner = rank <= 2 * both_sides
        distance = jnp.where(inner, (rank + 1) // 2, rank - both_sides)
        leftward = jnp.where(inner, rank % 2 == 1, left > right)
        return jnp.where(leftward, me - distance, me + distance)

    peers = [near(rank) for rank in range(1, n_s)]

    barrier = pltpu.get_barrier_semaphore()
    for offset in range(1, n_s):
        pl.semaphore_signal(
            barrier, inc=1, device_id={"space": lax.rem(me + offset, n_s)},
            device_id_type=pl.DeviceIdType.MESH,
        )
    for turn in range(1, n_t):
        pl.semaphore_signal(
            barrier, inc=1, device_id={"tm": lax.rem(mine + turn, n_t)},
            device_id_type=pl.DeviceIdType.MESH,
        )
    for piece in range(pieces):
        begin[me, pl.ds(piece, 6, stride=pieces), :] = start_ref[:, piece * lanes : (piece + 1) * lanes]
    pl.semaphore_wait(barrier, n_s - 1 + n_t - 1)

    def node_copy(peer, slot):
        return remote(nodes_ref, gathered.at[slot], send_a.at[peer], recv_a.at[slot], {"space": peer})

    def start_copy(peer, slot):
        return remote(begin.at[me], begin.at[slot], send_b.at[peer], recv_b.at[slot], {"space": peer})

    for peer in peers:
        node_copy(peer, me).start()
    for peer in reversed(peers):
        start_copy(peer, me).start()

    per_tile = lanes // CLUSTER
    inside = lax.broadcasted_iota(jnp.int32, (lanes, lanes), 0) // CLUSTER
    wanted = lax.broadcasted_iota(jnp.int32, (lanes, lanes), 1) % per_tile
    pool[...] = jnp.where(inside == wanted, 1.0, 0.0).astype(jnp.bfloat16)
    tile_of = lax.broadcasted_iota(jnp.int32, (CLUSTER, lanes), 0)
    owner = lax.broadcasted_iota(jnp.int32, (CLUSTER, lanes), 1) // per_tile
    merged[...] = jnp.where(tile_of == owner, 1.0, 0.0)
    for one in range(sources.shape[0]):
        prepare_source(sources.at[one], pieces)
    for one in range(targets.shape[0]):
        prepare_target(targets.at[one], pieces)
    for one in range(many_source.shape[0]):
        prepare_source(many_source.at[one], cluster_tiles)
    prepare_target(many_target, tiles)

    def coarse_sources(blocks, slot):
        count = blocks[0].shape[0] // 6
        parts = [part for block in blocks for part in split_three(block)]
        got = product(jnp.concatenate(parts, axis=0).astype(jnp.bfloat16), pool[...])
        size = 6 * count
        sums = []
        for at in range(0, got.shape[0], 3 * size):
            sums.append(got[at : at + size] + got[at + size : at + 2 * size] + got[at + 2 * size : at + 3 * size])
        state = []
        for one in range(6):
            tops = []
            for first in range(0, tiles, CLUSTER):
                total_of = None
                for tile in range(first, min(first + CLUSTER, tiles), min(count, CLUSTER)):
                    block, inner = sums[tile // count], tile % count
                    width = min(count, CLUSTER)
                    shift = tile - first
                    kept = (
                        block[one * count + inner : one * count + inner + width]
                        * merged[shift : shift + width, :]
                    )
                    kept = jnp.sum(kept, axis=0, keepdims=True)
                    total_of = kept if total_of is None else total_of + kept
                tops.append(total_of)
            whole = tops[0] if len(tops) == 1 else jnp.concatenate(tops, axis=0)
            state.append(whole * (1.0 / CLUSTER) if one < 3 else whole)
        return source_operands(many_source.at[slot], state, cluster_tiles)

    own = [comps(nodes_ref, node * rows) for node in range(3)]
    spots = [target_operand(targets.at[node], own[node], pieces) for node in range(3)]
    for rank in range(n_s):
        if rank > 0:
            source = peers[rank - 1]
            node_copy(source, source).wait_recv()
        groups = []
        for node in range(3):
            state = comps(gathered.at[source], node * rows) if rank > 0 else own[node]
            operands = source_operands(sources.at[rank * 3 + node], state, pieces)
            groups.append(cut(operands, spots[node], node == 1))
        for node, got in enumerate(run(kept, groups)):
            if rank == 0:
                sums[node] = got
            elif rank < n_s - 1:
                sums[node] = sums[node] + got
            else:
                put_sums(totals.at[node], sums[node] + got, 0, pieces)

    def node_blocks(node):
        part = pl.ds(node * rows, rows)
        return [nodes_ref[part, :]] + [gathered[peer, part, :] for peer in peers]

    fine = [
        finish(totals.at[node], comps(nodes_ref, node * rows), coupling, pieces) for node in range(3)
    ]

    def coarse_value(blocks, slot, spot, state, both):
        put_sums(totals.at[3 + slot], whole_sums(*coarse_sources(blocks, slot), spot, both), 0, pieces)
        return finish(totals.at[3 + slot], state, coupling, pieces)

    coarse_first = coarse_value(node_blocks(0), 0, spots[0], comps(nodes_ref), True)
    for one in range(6):
        steps[mine, me, one * pieces : (one + 1) * pieces, :] = step_length * (
            (fine[0][one] + 4.0 * fine[1][one] + fine[2][one]) / 6.0 - coarse_first[one]
        )

    def step_copy(turn, peer, slice_in, place_in):
        return remote(
            steps.at[slice_in, place_in], steps.at[slice_in, place_in],
            send_e.at[turn, peer], recv_e.at[slice_in, place_in], {"tm": turn, "space": peer},
        )

    def hand_out():
        def to_slice(count, carry):
            turn = n_t - 1 - count
            for peer in peers:
                step_copy(turn, peer, mine, me).start()
            step_copy(turn, me, mine, me).start()
            return carry

        lax.fori_loop(0, n_t - 1 - mine, to_slice, 0)
        for peer in peers:
            step_copy(mine, peer, mine, me).start()

    early = n_t // 4

    @pl.when(mine < early)
    def _():
        hand_out()

    def spread_state(step):
        return [history[step, one * tiles : (one + 1) * tiles, :] for one in range(6)]

    def history_blocks(step):
        return [history[step]]

    def coarse_step(step):
        operands = coarse_sources(history_blocks(step), 2)
        state = spread_state(step)
        spot = target_operand(many_target, state, tiles)
        groups = [
            cut(operands, spot[:, z * length : (z + 1) * length], True) for z in range(n_s)
        ]
        for z, got in enumerate(run_values(groups)):
            put_sums(many_total, got, z * pieces, tiles)
        value = finish(many_total, state, coupling, tiles)
        for one in range(6):
            coarse[step, one * tiles : (one + 1) * tiles, :] = value[one]

    def advance(step):
        for one in range(6):
            for z in range(n_s):
                at = one * tiles + z * pieces
                history[step + 1, at : at + pieces, :] = (
                    history[step, at : at + pieces, :]
                    + step_length * coarse[step, at : at + pieces, :]
                    + steps[step, z, one * pieces : (one + 1) * pieces, :]
                )

    def block(ref, step, place):
        return [
            ref[step, pl.ds(one * tiles + place * pieces, pieces), :] for one in range(6)
        ]

    for peer in peers:
        start_copy(peer, peer).wait_recv()
    for z in range(n_s):
        for one in range(6):
            at = one * tiles + z * pieces
            history[0, at : at + pieces, :] = begin[z, one * pieces : (one + 1) * pieces, :]
    coarse_last = coarse_value(node_blocks(2), 1, spots[2], comps(nodes_ref, 2 * rows), False)

    @pl.when(mine >= early)
    def _():
        hand_out()

    coarse_step(0)

    def chain_step(step, carry):
        for z in range(n_s):
            step_copy(mine, me, step, z).wait_recv()
        advance(step)
        coarse_step(step + 1)
        return carry

    lax.fori_loop(0, mine, chain_step, 0)
    for peer in peers:
        step_copy(mine, me, mine, peer).wait_recv()
    advance(mine)

    initial = block(history, mine, me)
    final_state = block(history, mine + 1, me)
    spot = target_operand(targets.at[3], final_state, pieces)
    coarse_end = coarse_value(history_blocks(mine + 1), 3, spot, final_state, False)
    first = block(coarse, mine, me)
    change_first = [first[one] - coarse_first[one] for one in range(6)]
    change_last = [coarse_end[one] - coarse_last[one] for one in range(6)]
    fixed_first = [fine[0][one] + change_first[one] for one in range(6)]
    fixed_middle = [fine[1][one] + 0.5 * (change_first[one] + change_last[one]) for one in range(6)]
    fixed_last = [fine[2][one] + change_last[one] for one in range(6)]

    spot = target_operand(targets.at[4], initial, pieces)
    groups = []
    for z in range(n_s):
        state = [
            history[mine, one * tiles + z * pieces : one * tiles + (z + 1) * pieces, :]
            for one in range(6)
        ]
        groups.append(cut(source_operands(sources.at[z], state, pieces), spot, False))
    put_sums(totals.at[0], functools.reduce(jnp.add, run(kept, groups)), 0, pieces)
    slope_first = finish(totals.at[0], initial, coupling, pieces)
    sweep_middle = [
        initial[one]
        + 0.5 * step_length * (slope_first[one] - fixed_first[one])
        + step_length * (5.0 * fixed_first[one] + 8.0 * fixed_middle[one] - fixed_last[one]) / 24.0
        for one in range(6)
    ]
    for one in range(6):
        middles[me, one * pieces : (one + 1) * pieces, :] = sweep_middle[one]

    def middle_copy(peer, slot):
        return remote(middles.at[me], middles.at[slot], send_w.at[peer], recv_w.at[slot], {"space": peer})

    for peer in reversed(peers):
        middle_copy(peer, me).start()
    half = 3 * pieces

    def write_out(node, state):
        for one in range(3):
            at = node * half + one * pieces
            places_out[at : at + pieces, :] = state[one]
            strengths_out[at : at + pieces, :] = state[3 + one]

    write_out(0, initial)
    write_out(1, sweep_middle)
    spot = target_operand(targets.at[5], sweep_middle, pieces)
    sums[1] = whole_sums(*source_operands(sources.at[n_s], sweep_middle, pieces), spot, False)
    for rank, peer in enumerate(peers):
        middle_copy(peer, peer).wait_recv()
        got = whole_sums(
            *source_operands(sources.at[n_s + 1 + rank], comps(middles.at[peer]), pieces), spot, False
        )
        if rank < n_s - 2:
            sums[1] = sums[1] + got
        else:
            put_sums(totals.at[1], sums[1] + got, 0, pieces)
    slope_middle = finish(totals.at[1], sweep_middle, coupling, pieces)
    sweep_last = [
        sweep_middle[one]
        + 0.5 * step_length * (slope_middle[one] - fixed_middle[one])
        + step_length * (-fixed_first[one] + 8.0 * fixed_middle[one] + 5.0 * fixed_last[one]) / 24.0
        for one in range(6)
    ]
    for one in range(6):
        handed[0, one * pieces : (one + 1) * pieces, :] = sweep_last[one]

    def last_copy():
        return remote(handed.at[0], handed.at[1], send_h, recv_h, {"tm": lax.rem(mine + 1, n_t)})

    @pl.when(mine < n_t - 1)
    def _():
        last_copy().start()

    write_out(2, sweep_last)
    for peer in peers:
        node_copy(peer, me).wait_send()
        start_copy(peer, me).wait_send()
        middle_copy(peer, me).wait_send()
        step_copy(mine, peer, mine, me).wait_send()

    def sent(turn, carry):
        for peer in range(n_s):
            step_copy(turn, peer, mine, me).wait_send()
        return carry

    lax.fori_loop(mine + 1, n_t, sent, 0)

    @pl.when(mine == 0)
    def _():
        next_places_out[...] = begin[me, 0:half, :]
        next_strengths_out[...] = begin[me, half : 2 * half, :]

    @pl.when(mine > 0)
    def _():
        last_copy().wait_recv()
        next_places_out[...] = handed[1, 0:half]
        next_strengths_out[...] = handed[1, half : 2 * half]

    @pl.when(mine < n_t - 1)
    def _():
        last_copy().wait_send()


def pass_on(*refs):
    count = len(refs) // 2
    for source, target in zip(refs[:count], refs[count:]):
        size = target.shape[1]
        for one in range(target.shape[0]):
            target[one] = source[one * size : (one + 1) * size, :]


def solution(mesh):
    n_t, n_s = mesh.shape["tm"], mesh.shape["space"]

    def shards(start_state, fine_nodes):
        length = start_state.shape[1]
        total = length * n_s
        vmem = pl.BlockSpec(memory_space=pltpu.VMEM)
        dma = pltpu.SemaphoreType.DMA
        lanes = math.gcd(length, 128)
        pieces = length // lanes
        tiles = n_s * pieces
        clusters = total // CLUSTER
        cluster_tiles = max(1, clusters // lanes)
        wide = min(clusters, lanes)

        def scratch(*shape):
            return pltpu.VMEM(shape, jnp.float32)

        made = pl.pallas_call(
            functools.partial(kernel, n_t, n_s),
            out_shape=tuple(
                jax.ShapeDtypeStruct((count * pieces, lanes), jnp.float32) for count in (9, 9, 3, 3)
            ),
            in_specs=[vmem, vmem],
            out_specs=(vmem, vmem, vmem, vmem),
            scratch_shapes=[
                scratch(n_s, 18 * pieces, lanes),
                scratch(n_s, 6 * pieces, lanes),
                scratch(3, SUM_ROWS, length),
                scratch(n_t, n_s, 6 * pieces, lanes),
                scratch(n_t + 1, 6 * tiles, lanes),
                scratch(n_t, 6 * tiles, lanes),
                scratch(n_s, 6 * pieces, lanes),
                scratch(2, 6 * pieces, lanes),
                pltpu.VMEM((lanes, lanes), jnp.bfloat16),
                scratch(CLUSTER, lanes),
                scratch(3 * n_s, SOURCE_ROWS * pieces, lanes),
                scratch(6, TARGET_ROWS * pieces, lanes),
                scratch(7, SUM_ROWS * pieces, lanes),
                scratch(4, SOURCE_ROWS * cluster_tiles, wide),
                scratch(TARGET_ROWS * tiles, lanes),
                scratch(SUM_ROWS * tiles, lanes),
                pltpu.VMEM((SLOTS, 4 * math.gcd(length, 256), length), jnp.bfloat16),
                dma((n_s,)), dma((n_s,)),
                dma((n_s,)), dma((n_s,)),
                dma((n_t, n_s)), dma((n_t, n_s)),
                dma((n_s,)), dma((n_s,)),
                dma, dma,
            ],
            compiler_params=pltpu.CompilerParams(collective_id=0, has_side_effects=True),
        )(start_state, fine_nodes.reshape(-1, lanes))
        made = pl.pallas_call(
            pass_on,
            out_shape=tuple(
                jax.ShapeDtypeStruct((count, pieces, lanes), jnp.float32) for count in (9, 9, 3, 3)
            ),
            in_specs=[vmem] * 4,
            out_specs=(vmem,) * 4,
        )(*made)
        nodes, ends = (1, 3, 3, length), (1, 3, length)
        return tuple(
            one.reshape(shape) for one, shape in zip(made, (nodes, nodes, ends, ends))
        )

    return jax.shard_map(
        shards,
        mesh=mesh,
        in_specs=(P(None, "space"), P("tm", None, None, "space")),
        out_specs=(
            P("tm", None, None, "space"),
            P("tm", None, None, "space"),
            P("tm", None, "space"),
            P("tm", None, "space"),
        ),
        check_vma=False,
    )
```

```python
import functools
import math

import jax
import jax.numpy as jnp
from jax import lax
from jax.experimental import pallas as pl
from jax.experimental.pallas import tpu as pltpu
from jax.sharding import PartitionSpec as P

CLUSTER = 16

core_squared = 0.01
step_length = 0.02


def rounded(value):
    return value.astype(jnp.bfloat16).astype(jnp.float32)


def split_three(value):
    one = rounded(value)
    two = rounded(value - one)
    return one, two, rounded(value - one - two)


def split_two(value):
    high = value.astype(jnp.bfloat16)
    return high, (value - high.astype(jnp.float32)).astype(jnp.bfloat16)


def product(left, right):
    return jnp.dot(left, right, preferred_element_type=jnp.float32)


def cross(left, right):
    return [
        left[1] * right[2] - left[2] * right[1],
        left[2] * right[0] - left[0] * right[2],
        left[0] * right[1] - left[1] * right[0],
    ]


def place_parts(state, extra):
    high = [rounded(one) for one in state[0:3]]
    low = [rounded(one - top) for one, top in zip(state[0:3], high)]
    used = [top + rest for top, rest in zip(high, low)]
    norm = used[0] * used[0] + used[1] * used[1] + used[2] * used[2] + extra
    return high, low, split_three(norm)


SLOTS = 4
SOURCE_ROWS = 56
TARGET_ROWS = 16
SUM_ROWS = 32


def write_rows(ref, first, values, tiles):
    for index, value in enumerate(values):
        ref[(first + index) * tiles : (first + index + 1) * tiles, :] = value


def read_rows(ref, first, count, tiles):
    if tiles == 1:
        return ref[first : first + count, :]
    return jnp.concatenate(
        [ref[pl.ds(first * tiles + tile, count, stride=tiles), :] for tile in range(tiles)], axis=1
    )


def constant_rows(ref, first, count, value, tiles):
    shape = (count * tiles, ref.shape[1])
    ref[first * tiles : (first + count) * tiles, :] = jnp.full(shape, value, jnp.float32)


def prepare_source(ref, tiles):
    constant_rows(ref, 9, 3, 1.0, tiles)
    constant_rows(ref, 12, 4, 0.0, tiles)
    constant_rows(ref, 22, 10, 0.0, tiles)


def prepare_target(ref, tiles):
    constant_rows(ref, 6, 3, 1.0, tiles)
    constant_rows(ref, 12, 4, 0.0, tiles)


def source_operands(ref, state, tiles):
    high, low, norm = place_parts(state, 0.0)
    base = state[3:6] + cross(state[0:3], state[3:6])
    write_rows(ref, 0, high + high + list(norm), tiles)
    write_rows(ref, 16, low + low, tiles)
    write_rows(ref, 32, base, tiles)
    for axis in range(3):
        write_rows(ref, 38 + 6 * axis, [state[axis] * one for one in base], tiles)
    places = read_rows(ref, 0, 32, tiles).astype(jnp.bfloat16)
    moments = read_rows(ref, 32, 24, tiles)
    high = rounded(moments)
    low = moments - high
    for_q = jnp.concatenate([high[0:8], low[0:8]], axis=0).astype(jnp.bfloat16)
    for_h = jnp.concatenate([high, low], axis=0).astype(jnp.bfloat16)
    return places, for_q, for_h


def target_operand(ref, state, tiles):
    high, low, norm = place_parts(state, core_squared)
    write_rows(ref, 0, [-2.0 * one for one in high] + [-2.0 * one for one in low], tiles)
    write_rows(ref, 9, norm, tiles)
    half = read_rows(ref, 0, TARGET_ROWS, tiles).astype(jnp.bfloat16)
    return jnp.concatenate([half, half], axis=0)


def spread_of(job):
    return lax.dot_general(
        job[0], job[3], (((0,), (0,)), ((), ())), preferred_element_type=jnp.float32
    )


def factors_of(job, spread):
    inverse = lax.rsqrt(spread)
    square = inverse * inverse
    factor = square * inverse
    steep = factor * square
    if job[4]:
        return (
            jnp.concatenate(split_two(factor), axis=0),
            jnp.concatenate(split_two(steep), axis=0),
        )
    return factor.astype(jnp.bfloat16), steep.astype(jnp.bfloat16)


def sums_from(job, factors):
    for_q, for_h = job[1], job[2]
    if job[4]:
        for_q = jnp.concatenate([for_q, for_q], axis=1)
        for_h = jnp.concatenate([for_h, for_h], axis=1)
    got_q = product(for_q, factors[0])
    got_h = product(for_h, factors[1])
    return jnp.concatenate([got_q[0:8] + got_q[8:16], got_h[0:24] + got_h[24:48]], axis=0)


def keep_factors(job, spread, kept, slot):
    inverse = lax.rsqrt(spread)
    square = inverse * inverse
    factor = square * inverse
    steep = factor * square
    rows = spread.shape[0]
    if job[4]:
        for part, value in ((0, factor), (2, steep)):
            high, low = split_two(value)
            kept[slot, part * rows : (part + 1) * rows, :] = high
            kept[slot, (part + 1) * rows : (part + 2) * rows, :] = low
    else:
        kept[slot, 0:rows, :] = factor.astype(jnp.bfloat16)
        kept[slot, 2 * rows : 3 * rows, :] = steep.astype(jnp.bfloat16)


def sums_of(job, kept, slot):
    for_q, for_h = job[1], job[2]
    rows = for_q.shape[1]
    if job[4]:
        for_q = jnp.concatenate([for_q, for_q], axis=1)
        for_h = jnp.concatenate([for_h, for_h], axis=1)
    got_q = product(for_q, kept[slot, 0 : for_q.shape[1], :])
    got_h = product(for_h, kept[slot, 2 * rows : 2 * rows + for_h.shape[1], :])
    return jnp.concatenate([got_q[0:8] + got_q[8:16], got_h[0:24] + got_h[24:48]], axis=0)


def cut(operands, target, both):
    places, for_q, for_h = operands
    length = places.shape[1]
    piece = math.gcd(length, 256)
    return [
        (places[:, at : at + piece], for_q[:, at : at + piece], for_h[:, at : at + piece], target, both)
        for at in range(0, length, piece)
    ]


def run(kept, groups):
    jobs = [job for group in groups for job in group]
    spreads, sums = {}, {}
    for turn in range(len(jobs) + 2):
        if turn < len(jobs):
            spreads[turn] = spread_of(jobs[turn])
        if 0 <= turn - 2:
            sums[turn - 2] = sums_of(jobs[turn - 2], kept, (turn - 2) % SLOTS)
        if 0 <= turn - 1 < len(jobs):
            keep_factors(jobs[turn - 1], spreads.pop(turn - 1), kept, (turn - 1) % SLOTS)
    results, at = [], 0
    for group in groups:
        total = sums[at]
        for more in range(at + 1, at + len(group)):
            total = total + sums[more]
        at += len(group)
        results.append(total)
    return results


def run_values(groups):
    jobs = [job for group in groups for job in group]
    spreads, factors, sums = {}, {}, {}
    for turn in range(len(jobs) + 2):
        if turn < len(jobs):
            spreads[turn] = spread_of(jobs[turn])
        if 0 <= turn - 2:
            sums[turn - 2] = sums_from(jobs[turn - 2], factors.pop(turn - 2))
        if 0 <= turn - 1 < len(jobs):
            factors[turn - 1] = factors_of(jobs[turn - 1], spreads.pop(turn - 1))
    results, at = [], 0
    for group in groups:
        total = sums[at]
        for more in range(at + 1, at + len(group)):
            total = total + sums[more]
        at += len(group)
        results.append(total)
    return results


def whole_sums(places, for_q, for_h, target, both=True):
    length = places.shape[1]
    piece = math.gcd(length, 256)
    parts_q, parts_h = [], []
    left_q, left_h = [], []
    for begin in range(0, length, piece):
        part = slice(begin, begin + piece)
        spread = lax.dot_general(
            places[:, part], target, (((0,), (0,)), ((), ())), preferred_element_type=jnp.float32
        )
        inverse = lax.rsqrt(spread)
        square = inverse * inverse
        factor = square * inverse
        steep = factor * square
        if both:
            parts_q.extend(split_two(factor))
            parts_h.extend(split_two(steep))
            left_q.extend([for_q[:, part]] * 2)
            left_h.extend([for_h[:, part]] * 2)
        else:
            parts_q.append(factor.astype(jnp.bfloat16))
            parts_h.append(steep.astype(jnp.bfloat16))
            left_q.append(for_q[:, part])
            left_h.append(for_h[:, part])

    def total(left, right):
        return product(jnp.concatenate(left, axis=1), jnp.concatenate(right, axis=0))

    got_q = total(left_q, parts_q)
    got_h = total(left_h, parts_h)
    return jnp.concatenate([got_q[0:8] + got_q[8:16], got_h[0:24] + got_h[24:48]], axis=0)


def put_sums(ref, sums, first, tiles):
    lanes = ref.shape[1]
    for tile in range(sums.shape[1] // lanes):
        ref[pl.ds(first + tile, SUM_ROWS, stride=tiles), :] = sums[:, tile * lanes : (tile + 1) * lanes]


def finish(ref, state, coupling, tiles):
    def row(index):
        return ref[index * tiles : (index + 1) * tiles, :]

    places, strengths = state[0:3], state[3:6]
    weighted = [row(index) for index in range(3)]
    turned = cross(places, weighted)
    velocity = [turned[index] - row(3 + index) for index in range(3)]
    along = strengths[0] * places[0] + strengths[1] * places[1] + strengths[2] * places[2]
    moment = [
        3.0
        * (
            along * row(8 + index)
            - strengths[0] * row(14 + index)
            - strengths[1] * row(20 + index)
            - strengths[2] * row(26 + index)
        )
        for index in range(6)
    ]
    bent = cross(places, moment[0:3])
    straight = cross(strengths, weighted)
    stretch = [straight[index] - (bent[index] - moment[3 + index]) for index in range(3)]
    return [-coupling * one for one in velocity + stretch]


def kernel(
    n_t,
    n_s,
    start_ref,
    nodes_ref,
    places_out,
    strengths_out,
    next_places_out,
    next_strengths_out,
    gathered,
    begin,
    sums,
    steps,
    history,
    coarse,
    middles,
    handed,
    pool,
    merged,
    sources,
    targets,
    totals,
    many_source,
    many_target,
    many_total,
    kept,
    send_a,
    recv_a,
    send_b,
    recv_b,
    send_e,
    recv_e,
    send_w,
    recv_w,
    send_h,
    recv_h,
):
    length = start_ref.shape[1]
    coupling = 1.0 / (4.0 * math.pi * math.sqrt(length * n_s))
    mine = lax.axis_index("tm")
    me = lax.axis_index("space")
    lanes = nodes_ref.shape[1]
    pieces = length // lanes
    rows = 6 * pieces
    tiles = n_s * pieces
    total = n_s * length
    clusters = total // CLUSTER
    cluster_tiles = max(1, clusters // lanes)

    def remote(source, target, send, recv, device):
        return pltpu.make_async_remote_copy(
            src_ref=source, dst_ref=target, send_sem=send, recv_sem=recv,
            device_id=device, device_id_type=pl.DeviceIdType.MESH,
        )

    def comps(ref, base=0):
        return [ref[base + one * pieces : base + (one + 1) * pieces, :] for one in range(6)]

    def near(rank):
        left, right = me, n_s - 1 - me
        both_sides = jnp.minimum(left, right)
        inner = rank <= 2 * both_sides
        distance = jnp.where(inner, (rank + 1) // 2, rank - both_sides)
        leftward = jnp.where(inner, rank % 2 == 1, left > right)
        return jnp.where(leftward, me - distance, me + distance)

    peers = [near(rank) for rank in range(1, n_s)]

    barrier = pltpu.get_barrier_semaphore()
    for offset in range(1, n_s):
        pl.semaphore_signal(
            barrier, inc=1, device_id={"space": lax.rem(me + offset, n_s)},
            device_id_type=pl.DeviceIdType.MESH,
        )
    for turn in range(1, n_t):
        pl.semaphore_signal(
            barrier, inc=1, device_id={"tm": lax.rem(mine + turn, n_t)},
            device_id_type=pl.DeviceIdType.MESH,
        )
    for piece in range(pieces):
        begin[me, pl.ds(piece, 6, stride=pieces), :] = start_ref[:, piece * lanes : (piece + 1) * lanes]
    pl.semaphore_wait(barrier, n_s - 1 + n_t - 1)

    def node_copy(peer, slot):
        return remote(nodes_ref, gathered.at[slot], send_a.at[peer], recv_a.at[slot], {"space": peer})

    def start_copy(peer, slot):
        return remote(begin.at[me], begin.at[slot], send_b.at[peer], recv_b.at[slot], {"space": peer})

    for peer in peers:
        node_copy(peer, me).start()
    for peer in reversed(peers):
        start_copy(peer, me).start()

    per_tile = lanes // CLUSTER
    inside = lax.broadcasted_iota(jnp.int32, (lanes, lanes), 0) // CLUSTER
    wanted = lax.broadcasted_iota(jnp.int32, (lanes, lanes), 1) % per_tile
    pool[...] = jnp.where(inside == wanted, 1.0, 0.0).astype(jnp.bfloat16)
    tile_of = lax.broadcasted_iota(jnp.int32, (CLUSTER, lanes), 0)
    owner = lax.broadcasted_iota(jnp.int32, (CLUSTER, lanes), 1) // per_tile
    merged[...] = jnp.where(tile_of == owner, 1.0, 0.0)
    for one in range(sources.shape[0]):
        prepare_source(sources.at[one], pieces)
    for one in range(targets.shape[0]):
        prepare_target(targets.at[one], pieces)
    for one in range(many_source.shape[0]):
        prepare_source(many_source.at[one], cluster_tiles)
    prepare_target(many_target, tiles)

    def coarse_sources(blocks, slot):
        count = blocks[0].shape[0] // 6
        parts = [part for block in blocks for part in split_three(block)]
        got = product(jnp.concatenate(parts, axis=0).astype(jnp.bfloat16), pool[...])
        size = 6 * count
        sums = []
        for at in range(0, got.shape[0], 3 * size):
            sums.append(got[at : at + size] + got[at + size : at + 2 * size] + got[at + 2 * size : at + 3 * size])
        state = []
        for one in range(6):
            tops = []
            for first in range(0, tiles, CLUSTER):
                total_of = None
                for tile in range(first, min(first + CLUSTER, tiles), min(count, CLUSTER)):
                    block, inner = sums[tile // count], tile % count
                    width = min(count, CLUSTER)
                    shift = tile - first
                    kept = (
                        block[one * count + inner : one * count + inner + width]
                        * merged[shift : shift + width, :]
                    )
                    kept = jnp.sum(kept, axis=0, keepdims=True)
                    total_of = kept if total_of is None else total_of + kept
                tops.append(total_of)
            whole = tops[0] if len(tops) == 1 else jnp.concatenate(tops, axis=0)
            state.append(whole * (1.0 / CLUSTER) if one < 3 else whole)
        return source_operands(many_source.at[slot], state, cluster_tiles)

    own = [comps(nodes_ref, node * rows) for node in range(3)]
    spots = [target_operand(targets.at[node], own[node], pieces) for node in range(3)]
    def node_blocks(node):
        part = pl.ds(node * rows, rows)
        return [nodes_ref[part, :]] + [gathered[peer, part, :] for peer in peers]

    for rank in range(n_s):
        if rank > 0:
            source = peers[rank - 1]
            node_copy(source, source).wait_recv()
        groups = []
        for node in range(3):
            state = comps(gathered.at[source], node * rows) if rank > 0 else own[node]
            operands = source_operands(sources.at[rank * 3 + node], state, pieces)
            groups.append(cut(operands, spots[node], node == 1))
        if rank == n_s - 1:
            groups.append(cut(coarse_sources(node_blocks(0), 0), spots[0], True))
        for node, got in enumerate(run(kept, groups)):
            if node == 3:
                put_sums(totals.at[3], got, 0, pieces)
            elif rank == 0:
                sums[node] = got
            elif rank < n_s - 1:
                sums[node] = sums[node] + got
            else:
                put_sums(totals.at[node], sums[node] + got, 0, pieces)

    fine = [
        finish(totals.at[node], comps(nodes_ref, node * rows), coupling, pieces) for node in range(3)
    ]

    def coarse_value(blocks, slot, spot, state, both):
        put_sums(totals.at[3 + slot], whole_sums(*coarse_sources(blocks, slot), spot, both), 0, pieces)
        return finish(totals.at[3 + slot], state, coupling, pieces)

    coarse_first = finish(totals.at[3], comps(nodes_ref), coupling, pieces)
    for one in range(6):
        steps[mine, me, one * pieces : (one + 1) * pieces, :] = step_length * (
            (fine[0][one] + 4.0 * fine[1][one] + fine[2][one]) / 6.0 - coarse_first[one]
        )

    def step_copy(turn, peer, slice_in, place_in):
        return remote(
            steps.at[slice_in, place_in], steps.at[slice_in, place_in],
            send_e.at[turn, peer], recv_e.at[slice_in, place_in], {"tm": turn, "space": peer},
        )

    def hand_out():
        def to_slice(count, carry):
            turn = n_t - 1 - count
            for peer in peers:
                step_copy(turn, peer, mine, me).start()
            step_copy(turn, me, mine, me).start()
            return carry

        lax.fori_loop(0, n_t - 1 - mine, to_slice, 0)
        for peer in peers:
            step_copy(mine, peer, mine, me).start()

    early = n_t // 4

    @pl.when(mine < early)
    def _():
        hand_out()

    def spread_state(step):
        return [history[step, one * tiles : (one + 1) * tiles, :] for one in range(6)]

    def history_blocks(step):
        return [history[step]]

    def coarse_step(step):
        operands = coarse_sources(history_blocks(step), 2)
        state = spread_state(step)
        spot = target_operand(many_target, state, tiles)
        groups = [
            cut(operands, spot[:, z * length : (z + 1) * length], True) for z in range(n_s)
        ]
        for z, got in enumerate(run_values(groups)):
            put_sums(many_total, got, z * pieces, tiles)
        value = finish(many_total, state, coupling, tiles)
        for one in range(6):
            coarse[step, one * tiles : (one + 1) * tiles, :] = value[one]

    def advance(step):
        for one in range(6):
            for z in range(n_s):
                at = one * tiles + z * pieces
                history[step + 1, at : at + pieces, :] = (
                    history[step, at : at + pieces, :]
                    + step_length * coarse[step, at : at + pieces, :]
                    + steps[step, z, one * pieces : (one + 1) * pieces, :]
                )

    def block(ref, step, place):
        return [
            ref[step, pl.ds(one * tiles + place * pieces, pieces), :] for one in range(6)
        ]

    for peer in peers:
        start_copy(peer, peer).wait_recv()
    for z in range(n_s):
        for one in range(6):
            at = one * tiles + z * pieces
            history[0, at : at + pieces, :] = begin[z, one * pieces : (one + 1) * pieces, :]
    coarse_last = coarse_value(node_blocks(2), 1, spots[2], comps(nodes_ref, 2 * rows), False)

    @pl.when(mine >= early)
    def _():
        hand_out()

    coarse_step(0)

    def chain_step(step, carry):
        for z in range(n_s):
            step_copy(mine, me, step, z).wait_recv()
        advance(step)
        coarse_step(step + 1)
        return carry

    lax.fori_loop(0, mine, chain_step, 0)
    for peer in peers:
        step_copy(mine, me, mine, peer).wait_recv()
    advance(mine)

    initial = block(history, mine, me)
    spot = target_operand(targets.at[4], initial, pieces)
    groups = []
    for z in range(n_s):
        state = [
            history[mine, one * tiles + z * pieces : one * tiles + (z + 1) * pieces, :]
            for one in range(6)
        ]
        groups.append(cut(source_operands(sources.at[z], state, pieces), spot, False))
    final_state = block(history, mine + 1, me)
    end_spot = target_operand(targets.at[3], final_state, pieces)
    groups.append(cut(coarse_sources(history_blocks(mine + 1), 3), end_spot, False))
    *got, end_sums = run(kept, groups)
    put_sums(totals.at[6], end_sums, 0, pieces)
    coarse_end = finish(totals.at[6], final_state, coupling, pieces)
    first = block(coarse, mine, me)
    change_first = [first[one] - coarse_first[one] for one in range(6)]
    change_last = [coarse_end[one] - coarse_last[one] for one in range(6)]
    fixed_first = [fine[0][one] + change_first[one] for one in range(6)]
    fixed_middle = [fine[1][one] + 0.5 * (change_first[one] + change_last[one]) for one in range(6)]
    fixed_last = [fine[2][one] + change_last[one] for one in range(6)]
    put_sums(totals.at[0], functools.reduce(jnp.add, got), 0, pieces)
    slope_first = finish(totals.at[0], initial, coupling, pieces)
    sweep_middle = [
        initial[one]
        + 0.5 * step_length * (slope_first[one] - fixed_first[one])
        + step_length * (5.0 * fixed_first[one] + 8.0 * fixed_middle[one] - fixed_last[one]) / 24.0
        for one in range(6)
    ]
    for one in range(6):
        middles[me, one * pieces : (one + 1) * pieces, :] = sweep_middle[one]

    def middle_copy(peer, slot):
        return remote(middles.at[me], middles.at[slot], send_w.at[peer], recv_w.at[slot], {"space": peer})

    for peer in reversed(peers):
        middle_copy(peer, me).start()
    half = 3 * pieces

    def write_out(node, state):
        for one in range(3):
            at = node * half + one * pieces
            places_out[at : at + pieces, :] = state[one]
            strengths_out[at : at + pieces, :] = state[3 + one]

    write_out(0, initial)
    write_out(1, sweep_middle)
    spot = target_operand(targets.at[5], sweep_middle, pieces)
    sums[1] = whole_sums(*source_operands(sources.at[n_s], sweep_middle, pieces), spot, False)
    for rank, peer in enumerate(peers):
        middle_copy(peer, peer).wait_recv()
        got = whole_sums(
            *source_operands(sources.at[n_s + 1 + rank], comps(middles.at[peer]), pieces), spot, False
        )
        if rank < n_s - 2:
            sums[1] = sums[1] + got
        else:
            put_sums(totals.at[1], sums[1] + got, 0, pieces)
    slope_middle = finish(totals.at[1], sweep_middle, coupling, pieces)
    sweep_last = [
        sweep_middle[one]
        + 0.5 * step_length * (slope_middle[one] - fixed_middle[one])
        + step_length * (-fixed_first[one] + 8.0 * fixed_middle[one] + 5.0 * fixed_last[one]) / 24.0
        for one in range(6)
    ]
    for one in range(6):
        handed[0, one * pieces : (one + 1) * pieces, :] = sweep_last[one]

    def last_copy():
        return remote(handed.at[0], handed.at[1], send_h, recv_h, {"tm": lax.rem(mine + 1, n_t)})

    @pl.when(mine < n_t - 1)
    def _():
        last_copy().start()

    write_out(2, sweep_last)
    for peer in peers:
        node_copy(peer, me).wait_send()
        start_copy(peer, me).wait_send()
        middle_copy(peer, me).wait_send()
        step_copy(mine, peer, mine, me).wait_send()

    def sent(turn, carry):
        for peer in range(n_s):
            step_copy(turn, peer, mine, me).wait_send()
        return carry

    lax.fori_loop(mine + 1, n_t, sent, 0)

    @pl.when(mine == 0)
    def _():
        next_places_out[...] = begin[me, 0:half, :]
        next_strengths_out[...] = begin[me, half : 2 * half, :]

    @pl.when(mine > 0)
    def _():
        last_copy().wait_recv()
        next_places_out[...] = handed[1, 0:half]
        next_strengths_out[...] = handed[1, half : 2 * half]

    @pl.when(mine < n_t - 1)
    def _():
        last_copy().wait_send()


def pass_on(*refs):
    count = len(refs) // 2
    for source, target in zip(refs[:count], refs[count:]):
        size = target.shape[1]
        for one in range(target.shape[0]):
            target[one] = source[one * size : (one + 1) * size, :]


def solution(mesh):
    n_t, n_s = mesh.shape["tm"], mesh.shape["space"]

    def shards(start_state, fine_nodes):
        length = start_state.shape[1]
        total = length * n_s
        vmem = pl.BlockSpec(memory_space=pltpu.VMEM)
        dma = pltpu.SemaphoreType.DMA
        lanes = math.gcd(length, 128)
        pieces = length // lanes
        tiles = n_s * pieces
        clusters = total // CLUSTER
        cluster_tiles = max(1, clusters // lanes)
        wide = min(clusters, lanes)

        def scratch(*shape):
            return pltpu.VMEM(shape, jnp.float32)

        made = pl.pallas_call(
            functools.partial(kernel, n_t, n_s),
            out_shape=tuple(
                jax.ShapeDtypeStruct((count * pieces, lanes), jnp.float32) for count in (9, 9, 3, 3)
            ),
            in_specs=[vmem, vmem],
            out_specs=(vmem, vmem, vmem, vmem),
            scratch_shapes=[
                scratch(n_s, 18 * pieces, lanes),
                scratch(n_s, 6 * pieces, lanes),
                scratch(3, SUM_ROWS, length),
                scratch(n_t, n_s, 6 * pieces, lanes),
                scratch(n_t + 1, 6 * tiles, lanes),
                scratch(n_t, 6 * tiles, lanes),
                scratch(n_s, 6 * pieces, lanes),
                scratch(2, 6 * pieces, lanes),
                pltpu.VMEM((lanes, lanes), jnp.bfloat16),
                scratch(CLUSTER, lanes),
                scratch(3 * n_s, SOURCE_ROWS * pieces, lanes),
                scratch(6, TARGET_ROWS * pieces, lanes),
                scratch(7, SUM_ROWS * pieces, lanes),
                scratch(4, SOURCE_ROWS * cluster_tiles, wide),
                scratch(TARGET_ROWS * tiles, lanes),
                scratch(SUM_ROWS * tiles, lanes),
                pltpu.VMEM((SLOTS, 4 * math.gcd(length, 256), length), jnp.bfloat16),
                dma((n_s,)), dma((n_s,)),
                dma((n_s,)), dma((n_s,)),
                dma((n_t, n_s)), dma((n_t, n_s)),
                dma((n_s,)), dma((n_s,)),
                dma, dma,
            ],
            compiler_params=pltpu.CompilerParams(collective_id=0, has_side_effects=True),
        )(start_state, fine_nodes.reshape(-1, lanes))
        made = pl.pallas_call(
            pass_on,
            out_shape=tuple(
                jax.ShapeDtypeStruct((count, pieces, lanes), jnp.float32) for count in (9, 9, 3, 3)
            ),
            in_specs=[vmem] * 4,
            out_specs=(vmem,) * 4,
        )(*made)
        nodes, ends = (1, 3, 3, length), (1, 3, length)
        return tuple(
            one.reshape(shape) for one, shape in zip(made, (nodes, nodes, ends, ends))
        )

    return jax.shard_map(
        shards,
        mesh=mesh,
        in_specs=(P(None, "space"), P("tm", None, None, "space")),
        out_specs=(
            P("tm", None, None, "space"),
            P("tm", None, None, "space"),
            P("tm", None, "space"),
            P("tm", None, "space"),
        ),
        check_vma=False,
    )
```
